32 devices in a mesh: step: 8 (over y, x, core), lat: 4 (over z).
Axes of the slice: x: 2, y: 2, z: 4, core: 2. Of those that a mesh axis runs over, the one named last changes fastest.
Arguments:
- state_in: bfloat16 [8, 72, 64, 128], P('step', None, 'lat'), may hold values from -6 to 6
- new_state: bfloat16 [72, 64, 128], P(None, 'lat'), may hold values from -6 to 6
- cot_early: bfloat16 [8, 72, 64, 128], P('step', None, 'lat'), may hold values from -6 to 6
- cot_late: bfloat16 [8, 72, 64, 128], P('step', None, 'lat'), may hold values from -6 to 6
- kernel_first: bfloat16 [9, 72, 192], replicated, may hold values from -0.25 to 0.25
- kernel_mid: bfloat16 [9, 192, 192], replicated, may hold values from -0.15625 to 0.15625
- kernel_last: bfloat16 [9, 72, 192], replicated, may hold values from -0.15625 to 0.15625
Outputs:
- advanced: bfloat16 [8, 72, 64, 128], P('step', None, 'lat')
- state_adjoint: bfloat16 [8, 72, 64, 128], P('step', None, 'lat')
- grad_first: float32 [9, 72, 192], replicated
- grad_mid: float32 [9, 192, 192], replicated
- grad_last: float32 [9, 72, 192], replicated
The draws below stay inside these ranges and needn't reach their ends.
All inputs are finite; a program needn't handle non-finite values.
Results may differ from the reference program's by a relative error of at most 0.008.
Values may be sent and summed in bfloat16 or wider, within the bound.
A program may use at most 64 MiB of HBM per device.

```python
import math
import jax
import jax.numpy as jnp
from jax import lax

CH = 72
HID = 192
COLS = 128
STEPS = 8
ROWS = 64


def levels(key, dims, pieces, smallest, high):
    gain = 1.0
    for axis_at, parts in pieces:
        heights = jax.random.uniform(jax.random.fold_in(jax.random.fold_in(key, 6), axis_at), (parts,), jnp.float32, smallest / len(pieces), high / len(pieces))
        gain = gain * jnp.repeat(jnp.exp(heights), dims[axis_at] // parts).reshape((-1,) + (1,) * (len(dims) - 1 - axis_at))
    return gain


def normal_values(own_key, dims, width, most, pieces=(), dtype=jnp.bfloat16):
    loudness = levels(own_key, dims, pieces, -0.22, 0.18) if pieces else 1.0
    entries = jax.random.normal(own_key, dims, jnp.float32) * width * loudness
    return jnp.minimum(jnp.maximum(entries, -most), most).astype(dtype)


def setup_inputs(seed: int = 0) -> dict:
    keys = jax.random.split(jax.random.key(seed), 8)
    return {
        "state_in": normal_values(keys[0], (STEPS, CH, ROWS, COLS), 1.0, 6.0, ((0, 8), (2, 4))),
        "new_state": normal_values(keys[1], (CH, ROWS, COLS), 1.0, 6.0, ((1, 4),)),
        "cot_early": normal_values(keys[2], (STEPS, CH, ROWS, COLS), 1.0, 6.0, ((0, 8), (2, 4))),
        "cot_late": normal_values(keys[3], (STEPS, CH, ROWS, COLS), 1.0, 6.0, ((0, 8), (2, 4))),
        "kernel_first": normal_values(keys[4], (9, CH, HID), (9 * CH) ** -0.5, 0.25),
        "kernel_mid": normal_values(keys[5], (9, HID, HID), (9 * HID) ** -0.5, 0.15625),
        "kernel_last": normal_values(keys[6], (9, CH, HID), (9 * HID) ** -0.5, 0.15625),
    }


def pad_rows(values, dilation):
    return jnp.pad(values, ((0, 0), (dilation, dilation), (0, 0)))

def window_at(padded, dilation, row_tap, col_tap, out_rows, out_cols):
    widened = jnp.pad(padded, ((0, 0), (0, 0), (dilation, dilation)))
    return widened[:, row_tap * dilation:row_tap * dilation + out_rows, col_tap * dilation:col_tap * dilation + out_cols]

def convolve(padded, kernel, dilation, flipped):
    out_rows = padded.shape[1] - 2 * dilation
    out_cols = padded.shape[2]
    pattern = 'oc,crw->orw' if flipped else 'co,crw->orw'
    summed = None
    for tap_index in range(9):
        window = window_at(padded, dilation, tap_index // 3, tap_index % 3, out_rows, out_cols)
        product = jnp.einsum(pattern, kernel[tap_index].astype(jnp.float32), window.astype(jnp.float32))
        summed = product if summed is None else summed + product
    return summed

def convolve_back(padded, kernel, dilation, flipped):
    out_rows = padded.shape[1] - 2 * dilation
    out_cols = padded.shape[2]
    pattern = 'oc,orw->crw' if flipped else 'co,orw->crw'
    summed = None
    for tap_index in range(9):
        window = window_at(padded, dilation, 2 - tap_index // 3, 2 - tap_index % 3, out_rows, out_cols)
        product = jnp.einsum(pattern, kernel[tap_index].astype(jnp.float32), window.astype(jnp.float32))
        summed = product if summed is None else summed + product
    return summed

def kernel_terms(padded_in, grad_out, dilation, flipped):
    out_rows = grad_out.shape[1]
    out_cols = grad_out.shape[2]
    pattern = 'crw,orw->oc' if flipped else 'crw,orw->co'
    listed = []
    for tap_index in range(9):
        window = window_at(padded_in, dilation, tap_index // 3, tap_index % 3, out_rows, out_cols)
        listed.append(jnp.einsum(pattern, window.astype(jnp.float32), grad_out.astype(jnp.float32)))
    return jnp.stack(listed)

def gelu_slope(preact, cotangent):
    return jax.vjp(jax.nn.gelu, preact)[1](cotangent)[0]

def advance(state, kernels):
    kernel_first, kernel_mid, kernel_last = kernels
    in_first = pad_rows(state, 1)
    pre_first = convolve(in_first, kernel_first, 1, False)
    hid_first = jax.nn.gelu(pre_first).astype(jnp.bfloat16)
    in_mid = pad_rows(hid_first, 2)
    pre_mid = convolve(in_mid, kernel_mid, 2, False)
    hid_mid = jax.nn.gelu(pre_mid).astype(jnp.bfloat16)
    in_last = pad_rows(hid_mid, 4)
    pre_last = convolve(in_last, kernel_last, 4, True)
    output = (state.astype(jnp.float32) + pre_last).astype(jnp.bfloat16)
    return (output, (in_first, in_mid, in_last, pre_first, pre_mid))

def backward(cot_out, saved, kernels):
    kernel_first, kernel_mid, kernel_last = kernels
    in_first, in_mid, in_last, pre_first, pre_mid = saved
    back_mid = convolve_back(pad_rows(cot_out, 4), kernel_last, 4, True)
    grads_last = kernel_terms(in_last, cot_out, 4, True)
    delta_mid = gelu_slope(pre_mid, back_mid).astype(jnp.bfloat16)
    back_first = convolve_back(pad_rows(delta_mid, 2), kernel_mid, 2, False)
    grads_mid = kernel_terms(in_mid, delta_mid, 2, False)
    delta_first = gelu_slope(pre_first, back_first).astype(jnp.bfloat16)
    back_state = convolve_back(pad_rows(delta_first, 1), kernel_first, 1, False)
    grads_first = kernel_terms(in_first, delta_first, 1, False)
    adjoint = (cot_out.astype(jnp.float32) + back_state).astype(jnp.bfloat16)
    return (adjoint, (grads_first, grads_mid, grads_last))

def reference(state_in, new_state, cot_early, cot_late, kernel_first, kernel_mid, kernel_last):
    kernels = (kernel_first, kernel_mid, kernel_last)

    def forward_only(state):
        return advance(state, kernels)[0]
    early = lax.map(forward_only, state_in)
    late_in = jnp.concatenate([new_state[None], early[:-1]], axis=0)

    def late_pass(pair):
        state, cotangent = pair
        output, saved = advance(state, kernels)
        adjoint, grads = backward(cotangent, saved, kernels)
        return (output, adjoint, grads)
    advanced, late_adj, late_grads = lax.map(late_pass, (late_in, cot_late))
    returned = jnp.concatenate([late_adj[1:], jnp.zeros_like(late_adj[:1])], axis=0)
    early_cot = (cot_early.astype(jnp.float32) + returned.astype(jnp.float32)).astype(jnp.bfloat16)

    def early_pass(pair):
        state, cotangent = pair
        output, saved = advance(state, kernels)
        return backward(cotangent, saved, kernels)
    state_adjoint, early_grads = lax.map(early_pass, (state_in, early_cot))
    grad_scale = 1.0 / math.sqrt(2.0 * STEPS * ROWS * COLS)
    grad_first = (lax.optimization_barrier(jnp.sum(late_grads[0], axis=0)) + lax.optimization_barrier(jnp.sum(early_grads[0], axis=0))) * grad_scale
    grad_mid = (lax.optimization_barrier(jnp.sum(late_grads[1], axis=0)) + lax.optimization_barrier(jnp.sum(early_grads[1], axis=0))) * grad_scale
    grad_last = (lax.optimization_barrier(jnp.sum(late_grads[2], axis=0)) + lax.optimization_barrier(jnp.sum(early_grads[2], axis=0))) * grad_scale
    return (advanced, state_adjoint, grad_first, grad_mid, grad_last)
```

```python
import functools
import math

import jax
import jax.numpy as jnp
from jax import lax
from jax.experimental import pallas as pl
from jax.experimental.pallas import tpu as pltpu
from jax.sharding import PartitionSpec as P

MESH = pl.DeviceIdType.MESH
BF = jnp.bfloat16
F32 = jnp.float32
HALO = 7
NT = (((1,), (1,)), ((), ()))


def gelu_pair(a):
    k = math.sqrt(2.0 / math.pi)
    sq = a * a
    t = jnp.tanh(k * (a + 0.044715 * (sq * a)))
    half = 0.5 * (1.0 + t)
    slope = half + (0.5 * a) * (1.0 - t * t) * (k * (1.0 + (3.0 * 0.044715) * sq))
    return a * half, slope


def spread(dst, value, lane, width, dilation, sign):
    channels = value.shape[0]
    column = lax.broadcasted_iota(jnp.int32, (channels, width), 1)
    for k in range(value.shape[1] // width):
        piece = value[:, k * width : (k + 1) * width]
        for j in range(3):
            shift = sign * dilation * (j - 1)
            if shift == 0:
                moved = piece
            else:
                moved = pltpu.roll(piece, (-shift) % width, 1)
                good = (column + shift >= 0) & (column + shift < width)
                moved = jnp.where(good, moved, 0.0)
            dst[j * channels : (j + 1) * channels, pl.ds(pl.multiple_of(lane + k * width, width), width)] = (
                moved.astype(BF)
            )


def conv_chunk(weights, src, row, dilation, width, back, first_row=0):
    total = None
    for i in range(3):
        offset = (2 - i if back else i) * dilation + first_row
        lane = pl.multiple_of((row + offset) * width, width)
        part = jnp.dot(weights[i], src[:, pl.ds(lane, 2 * width)], preferred_element_type=F32)
        total = part if total is None else total + part
    return total


def forward_part(rows, width, x, mask, w1, w2, w3, out, v3, h1, h2, s1, s2, h1s, h2s):
    chunk = 2 * width
    channels = x.shape[0]

    def lanes(row):
        return pl.ds(pl.multiple_of(row * width, width), chunk)

    @pl.loop(0, (rows + 14) // 2)
    def _(c):
        spread(v3, x[:, lanes(2 * c)].astype(F32), 2 * c * width, width, 1, 1)

    @pl.loop(0, (rows + 12) // 2)
    def _(c):
        value, slope = gelu_pair(conv_chunk(w1, v3, 2 * c, 1, width, False))
        value = jnp.where(mask[:, lanes(2 * c + 1)] > 0, value, 0.0).astype(BF)
        h1[:, lanes(2 * c)] = value
        s1[:, lanes(2 * c)] = slope
        spread(h1s, value.astype(F32), 2 * c * width, width, 2, 1)

    @pl.loop(0, (rows + 8) // 2)
    def _(c):
        value, slope = gelu_pair(conv_chunk(w2, h1s, 2 * c, 2, width, False))
        value = jnp.where(mask[:, lanes(2 * c + 3)] > 0, value, 0.0).astype(BF)
        h2[:, lanes(2 * c)] = value
        s2[:, lanes(2 * c)] = slope
        spread(h2s, value.astype(F32), 2 * c * width, width, 4, 1)

    @pl.loop(0, rows // 2)
    def _(c):
        total = conv_chunk(w3, h2s, 2 * c, 4, width, False)
        base = x[:, lanes(2 * c + HALO)].astype(F32)
        out[:, lanes(2 * c)] = (base + total).astype(BF)


def backward_part(rows, width, cot, mask, w1b, w2b, w3b, v3, h1, h2, s1, s2, adj, tf, tm, tl, c3, g2s, g1s):
    chunk = 2 * width
    band = rows * width

    def lanes(row):
        return pl.ds(pl.multiple_of(row * width, width), chunk)

    @pl.loop(0, (rows + 14) // 2)
    def _(c):
        spread(c3, cot[:, lanes(2 * c)].astype(F32), 2 * c * width, width, 4, -1)

    @pl.loop(0, (rows + 6) // 2)
    def _(c):
        total = conv_chunk(w3b, c3, 2 * c, 4, width, True)
        delta = s2[:, lanes(2 * c + 1)] * total
        delta = jnp.where(mask[:, lanes(2 * c + 4)] > 0, delta, 0.0).astype(BF)
        spread(g2s, delta.astype(F32), 2 * c * width, width, 2, -1)

    @pl.loop(0, (rows + 2) // 2)
    def _(c):
        total = conv_chunk(w2b, g2s, 2 * c, 2, width, True)
        delta = s1[:, lanes(2 * c + 5)] * total
        delta = jnp.where(mask[:, lanes(2 * c + 6)] > 0, delta, 0.0).astype(BF)
        spread(g1s, delta.astype(F32), 2 * c * width, width, 1, -1)

    @pl.loop(0, rows // 2)
    def _(c):
        total = conv_chunk(w1b, g1s, 2 * c, 1, width, True)
        base = cot[:, lanes(2 * c + HALO)].astype(F32)
        adj[:, lanes(2 * c)] = (base + total).astype(BF)

    hid = h1.shape[0]

    def nt(a, b):
        return lax.dot_general(a, b, NT, preferred_element_type=F32)

    @pl.loop(0, 3)
    def _(i):
        def window(row):
            return pl.ds(pl.multiple_of(row * width, width), band)

        tl[i] = nt(c3[:, window(3 + (2 - i) * 4)], h2[:, 4 * width : 4 * width + band])
        tf[i] = nt(v3[:, window(6 + i)], g1s[hid : 2 * hid, width : width + band])
        for j in range(3):
            tm[i, j] = nt(
                h1[:, 6 * width : 6 * width + band],
                g2s[j * hid : (j + 1) * hid, window(1 + (2 - i) * 2)],
            )


def early_forward_kernel(rows, width, x, mask, w1, w2, w3, out, v3, h1, h2, s1, s2, h1s, h2s):
    forward_part(rows, width, x, mask, w1, w2, w3, out, v3, h1, h2, s1, s2, h1s, h2s)


def late_kernel(
    rows, width, x, cot, mask, w1, w2, w3, w1b, w2b, w3b, out, adj, tf, tm, tl,
    v3, h1, h2, s1, s2, h1s, h2s, c3, g2s, g1s,
):
    forward_part(rows, width, x, mask, w1, w2, w3, out, v3, h1, h2, s1, s2, h1s, h2s)
    backward_part(rows, width, cot, mask, w1b, w2b, w3b, v3, h1, h2, s1, s2, adj, tf, tm, tl, c3, g2s, g1s)


def early_backward_kernel(
    rows, width, cot, mask, w1b, w2b, w3b, v3, h1, h2, s1, s2, adj, tf, tm, tl, c3, g2s, g1s
):
    backward_part(rows, width, cot, mask, w1b, w2b, w3b, v3, h1, h2, s1, s2, adj, tf, tm, tl, c3, g2s, g1s)


def reduce_kernel(pairs, lats, scale, src, out, got_a, part_b, got_b, part_c, got_c, full, send, recv):
    step = lax.axis_index("step")
    lat = lax.axis_index("lat")
    core = lax.rem(step, 2)
    pair = step // 2

    partner = {"step": pair * 2 + (1 - core)}

    def pair_peer(k):
        return {"step": lax.rem(pair + k, pairs) * 2 + core}

    def lat_peer(k):
        return {"lat": lax.rem(lat + k, lats)}

    peers = [partner]
    peers += [pair_peer(k) for k in range(1, pairs)]
    peers += [lat_peer(k) for k in range(1, lats)]
    barrier = pltpu.get_barrier_semaphore()
    for peer in peers:
        pl.semaphore_signal(barrier, inc=1, device_id=peer, device_id_type=MESH)
    pl.semaphore_wait(barrier, len(peers))

    count = [0]

    def copy(source, target, peer):
        slot = count[0]
        count[0] += 1
        made = pltpu.make_async_remote_copy(
            src_ref=source, dst_ref=target, send_sem=send.at[slot], recv_sem=recv.at[slot],
            device_id=peer, device_id_type=MESH,
        )
        made.start()
        return made

    def finish(copies):
        for made in copies:
            made.wait()

    finish([copy(src.at[1 - core], got_a, partner)])
    for b in range(pairs):
        part_b[b] = (src[core, b].astype(F32) + got_a[b].astype(F32)).astype(BF)
    finish([copy(part_b.at[lax.rem(pair + k, pairs)], got_b.at[k - 1], pair_peer(k)) for k in range(1, pairs)])
    for c in range(lats):
        total = src[core, pair, c].astype(F32) + got_a[pair, c].astype(F32)
        for k in range(pairs - 1):
            total = total + got_b[k, c].astype(F32)
        part_c[c] = total.astype(BF)
    finish([copy(part_c.at[lax.rem(lat + k, lats)], got_c.at[k - 1], lat_peer(k)) for k in range(1, lats)])
    total = part_c[lat].astype(F32)
    for k in range(lats - 1):
        total = total + got_c[k].astype(F32)
    full[core, pair, lat] = (total * scale).astype(BF)
    piece = full.at[core, pair, lat]
    finish([copy(piece, piece, lat_peer(k)) for k in range(1, lats)])
    piece = full.at[core, pair]
    finish([copy(piece, piece, pair_peer(k)) for k in range(1, pairs)])
    piece = full.at[core]
    finish([copy(piece, piece, partner)])
    for a in range(2):
        for b in range(pairs):
            out[a, b] = full[a, b].astype(F32)


def all_reduce(values, scale):
    pairs = lax.axis_size("step") // 2
    lats = lax.axis_size("lat")
    pieces = 2 * pairs * lats
    total, width = values.shape
    piece = -(-total // (pieces * 16)) * 16
    src = jnp.pad(values, ((0, piece * pieces - total), (0, 0))).reshape(2, pairs, lats, piece, width)
    copies = 2 + 2 * (pairs - 1) + 2 * (lats - 1)
    vmem = pl.BlockSpec(memory_space=pltpu.VMEM)
    out = pl.pallas_call(
        functools.partial(reduce_kernel, pairs, lats, scale),
        out_shape=jax.ShapeDtypeStruct(src.shape, F32),
        in_specs=[vmem],
        out_specs=vmem,
        scratch_shapes=[
            pltpu.VMEM((pairs, lats, piece, width), BF),
            pltpu.VMEM((pairs, lats, piece, width), BF),
            pltpu.VMEM((max(pairs - 1, 1), lats, piece, width), BF),
            pltpu.VMEM((lats, piece, width), BF),
            pltpu.VMEM((max(lats - 1, 1), piece, width), BF),
            pltpu.VMEM(src.shape, BF),
            pltpu.SemaphoreType.DMA((copies,)),
            pltpu.SemaphoreType.DMA((copies,)),
        ],
        compiler_params=pltpu.CompilerParams(collective_id=0, has_side_effects=True),
        name="kernel_term_sum",
    )(src)
    return out.reshape(pieces * piece, width)[:total]


def body(state_in, new_state, cot_early, cot_late, kernel_first, kernel_mid, kernel_last):
    steps, lats = lax.axis_size("step"), lax.axis_size("lat")
    ch, rows, width = new_state.shape
    hid = kernel_mid.shape[1]
    cp = -(-ch // 16) * 16
    band, edge = rows * width, HALO * width
    lat = lax.axis_index("lat")
    step = lax.axis_index("step")

    grid_first = jnp.pad(kernel_first.reshape(3, 3, ch, hid), ((0, 0), (0, 0), (0, cp - ch), (0, 0)))
    grid_last = jnp.pad(kernel_last.reshape(3, 3, ch, hid), ((0, 0), (0, 0), (0, cp - ch), (0, 0)))
    grid_mid = kernel_mid.reshape(3, 3, hid, hid)
    w1 = grid_first.transpose(0, 3, 1, 2).reshape(3, hid, 3 * cp)
    w2 = grid_mid.transpose(0, 3, 1, 2).reshape(3, hid, 3 * hid)
    w3 = grid_last.transpose(0, 2, 1, 3).reshape(3, cp, 3 * hid)
    w1b = grid_first.transpose(0, 2, 1, 3).reshape(3, cp, 3 * hid)
    w2b = grid_mid.transpose(0, 2, 1, 3).reshape(3, hid, 3 * hid)
    w3b = grid_last.transpose(0, 3, 1, 2).reshape(3, hid, 3 * cp)

    ext_row = lat * rows + jnp.arange(rows + 2 * HALO, dtype=jnp.int32) - HALO
    inside = (ext_row >= 0) & (ext_row < rows * lats)
    mask = jnp.repeat(inside.astype(F32), width)[None]

    packed = jnp.stack([state_in[0], new_state, cot_late[0], cot_early[0]]).reshape(4, ch, band)
    low = lax.ppermute(packed[:, :, band - edge :], "lat", [(i, i + 1) for i in range(lats - 1)])
    high = lax.ppermute(packed[:, :, :edge], "lat", [(i + 1, i) for i in range(lats - 1)])
    wide = jnp.concatenate([low, packed, high], axis=2)
    wide = jnp.pad(wide, ((0, 0), (0, cp - ch), (0, 0)))
    state_w, new_w, late_cot_w, early_cot_w = wide[0], wide[1], wide[2], wide[3]

    def to_step(block, distance):
        def send(part, lat_shift):
            route = []
            for s in range(steps):
                for l in range(lats):
                    if 0 <= s + distance < steps and 0 <= l + lat_shift < lats:
                        route.append((s * lats + l, (s + distance) * lats + l + lat_shift))
            return lax.ppermute(part, ("step", "lat"), route)

        trimmed = block[:ch]
        joined = jnp.concatenate(
            [send(trimmed[:, band - edge :], 1), send(trimmed, 0), send(trimmed[:, :edge], -1)], axis=1
        )
        return jnp.pad(joined, ((0, cp - ch), (0, 0)))

    vmem = pl.BlockSpec(memory_space=pltpu.VMEM)
    shape = jax.ShapeDtypeStruct
    lanes_v, lanes_1, lanes_2 = (rows + 14) * width, (rows + 12) * width, (rows + 8) * width
    saved_shapes = [
        ((3 * cp, lanes_v), BF), ((hid, lanes_1), BF), ((hid, lanes_2), BF),
        ((hid, lanes_1), F32), ((hid, lanes_2), F32),
    ]
    fwd_scratch = [((3 * hid, lanes_1), BF), ((3 * hid, lanes_2), BF)]
    bwd_scratch = [
        ((3 * cp, lanes_v), BF), ((3 * hid, (rows + 6) * width), BF), ((3 * hid, (rows + 2) * width), BF)
    ]
    bwd_outs = [
        ((cp, band), BF), ((3, 3 * cp, hid), F32), ((3, 3, hid, hid), F32), ((3, 3 * cp, hid), F32)
    ]

    def call(kernel, name, ins, outs, scratch):
        return pl.pallas_call(
            functools.partial(kernel, rows, width),
            out_shape=[shape(*o) for o in outs],
            in_specs=[vmem] * len(ins),
            out_specs=[vmem] * len(outs),
            scratch_shapes=[pltpu.VMEM(*s) for s in scratch],
            compiler_params=pltpu.CompilerParams(vmem_limit_bytes=56 * 1024 * 1024),
            name=name,
        )(*ins)

    early_out, *saved = call(
        early_forward_kernel, "early_forward", (state_w, mask, w1, w2, w3),
        [((cp, band), BF)] + saved_shapes, fwd_scratch,
    )
    late_in = jnp.where(step == 0, new_w, to_step(early_out, 1))
    late_out, late_adj, *late_terms = call(
        late_kernel, "late_both", (late_in, late_cot_w, mask, w1, w2, w3, w1b, w2b, w3b),
        [((cp, band), BF)] + bwd_outs, saved_shapes + fwd_scratch + bwd_scratch,
    )
    early_cot = (early_cot_w.astype(F32) + to_step(late_adj, -1).astype(F32)).astype(BF)
    state_adj, *early_terms = call(
        early_backward_kernel, "early_backward", (early_cot, mask, w1b, w2b, w3b, *saved),
        bwd_outs, bwd_scratch,
    )

    first, mid, last = (a + b for a, b in zip(late_terms, early_terms))
    first = first.reshape(9, cp, hid)[:, :ch].reshape(9 * ch, hid)
    last = last.reshape(9, cp, hid)[:, :ch].reshape(9 * ch, hid)
    terms = jnp.concatenate([first, mid.reshape(9 * hid, hid), last]).astype(BF)
    n_terms, lane = terms.shape[0], 128
    left, tail = terms[:, :lane], terms[:, lane:]
    fold = lane // tail.shape[1]
    share = n_terms // fold
    folded = jnp.concatenate([tail[k * share : (k + 1) * share] for k in range(fold)], axis=1)
    scale = 1.0 / math.sqrt(2.0 * steps * rows * lats * width)
    summed = all_reduce(jnp.concatenate([left, folded]), scale)
    folded = summed[n_terms:]
    size = hid - lane
    tail = jnp.concatenate([folded[:, k * size : (k + 1) * size] for k in range(fold)], axis=0)
    summed = jnp.concatenate([summed[:n_terms], tail], axis=1)
    return (
        late_out[:ch].reshape(1, ch, rows, width),
        state_adj[:ch].reshape(1, ch, rows, width),
        summed[: 9 * ch].reshape(9, ch, hid),
        summed[9 * ch : 9 * ch + 9 * hid].reshape(9, hid, hid),
        summed[9 * ch + 9 * hid :].reshape(9, ch, hid),
    )


def solution(mesh):
    banded = P("step", None, "lat", None)
    return jax.shard_map(
        body,
        mesh=mesh,
        in_specs=(banded, P(None, "lat", None), banded, banded, P(), P(), P()),
        out_specs=(banded, banded, P(), P(), P()),
        check_vma=False,
    )
```

```python
import functools
import math

import jax
import jax.numpy as jnp
from jax import lax
from jax.experimental import pallas as pl
from jax.experimental.pallas import tpu as pltpu
from jax.sharding import PartitionSpec as P

MESH = pl.DeviceIdType.MESH
BF = jnp.bfloat16
F32 = jnp.float32
HALO = 7
NT = (((1,), (1,)), ((), ()))


def gelu_pair(a):
    k = math.sqrt(2.0 / math.pi)
    sq = a * a
    t = jnp.tanh(k * (a + 0.044715 * (sq * a)))
    half = 0.5 * (1.0 + t)
    slope = half + (0.5 * a) * (1.0 - t * t) * (k * (1.0 + (3.0 * 0.044715) * sq))
    return a * half, slope


def spread(dst, value, lane, width, dilation, sign):
    channels = value.shape[0]
    column = lax.broadcasted_iota(jnp.int32, (channels, width), 1)
    for k in range(value.shape[1] // width):
        piece = value[:, k * width : (k + 1) * width]
        for j in range(3):
            shift = sign * dilation * (j - 1)
            if shift == 0:
                moved = piece
            else:
                moved = pltpu.roll(piece, (-shift) % width, 1)
                good = (column + shift >= 0) & (column + shift < width)
                moved = jnp.where(good, moved, 0.0)
            dst[j * channels : (j + 1) * channels, pl.ds(pl.multiple_of(lane + k * width, width), width)] = (
                moved.astype(BF)
            )


def conv_chunk(weights, src, row, dilation, width, back, first_row=0):
    windows = []
    for i in range(3):
        offset = (2 - i if back else i) * dilation + first_row
        lane = pl.multiple_of((row + offset) * width, width)
        windows.append(src[:, pl.ds(lane, 2 * width)])
    return jnp.dot(weights[...], jnp.concatenate(windows, axis=0), preferred_element_type=F32)


def forward_part(rows, width, x, mask, w1, w2, w3, out, v3, h1, h2, s1, s2, h1s, h2s):
    chunk = 2 * width
    channels = x.shape[0]

    def lanes(row):
        return pl.ds(pl.multiple_of(row * width, width), chunk)

    @pl.loop(0, (rows + 14) // 2)
    def _(c):
        spread(v3, x[:, lanes(2 * c)].astype(F32), 2 * c * width, width, 1, 1)

    @pl.loop(0, (rows + 12) // 2)
    def _(c):
        value, slope = gelu_pair(conv_chunk(w1, v3, 2 * c, 1, width, False))
        value = jnp.where(mask[:, lanes(2 * c + 1)] > 0, value, 0.0).astype(BF)
        h1[:, lanes(2 * c)] = value
        s1[:, lanes(2 * c)] = slope
        spread(h1s, value.astype(F32), 2 * c * width, width, 2, 1)

    @pl.loop(0, (rows + 8) // 2)
    def _(c):
        value, slope = gelu_pair(conv_chunk(w2, h1s, 2 * c, 2, width, False))
        value = jnp.where(mask[:, lanes(2 * c + 3)] > 0, value, 0.0).astype(BF)
        h2[:, lanes(2 * c)] = value
        s2[:, lanes(2 * c)] = slope
        spread(h2s, value.astype(F32), 2 * c * width, width, 4, 1)

    @pl.loop(0, rows // 2)
    def _(c):
        total = conv_chunk(w3, h2s, 2 * c, 4, width, False)
        base = x[:, lanes(2 * c + HALO)].astype(F32)
        out[:, lanes(2 * c)] = (base + total).astype(BF)


def backward_part(rows, width, cot, mask, w1b, w2b, w3b, v3, h1, h2, s1, s2, adj, tf, tm, tl, c3, g2s, g1s):
    chunk = 2 * width
    band = rows * width

    def lanes(row):
        return pl.ds(pl.multiple_of(row * width, width), chunk)

    @pl.loop(0, (rows + 14) // 2)
    def _(c):
        spread(c3, cot[:, lanes(2 * c)].astype(F32), 2 * c * width, width, 4, -1)

    @pl.loop(0, (rows + 6) // 2)
    def _(c):
        total = conv_chunk(w3b, c3, 2 * c, 4, width, True)
        delta = s2[:, lanes(2 * c + 1)] * total
        delta = jnp.where(mask[:, lanes(2 * c + 4)] > 0, delta, 0.0).astype(BF)
        spread(g2s, delta.astype(F32), 2 * c * width, width, 2, -1)

    @pl.loop(0, (rows + 2) // 2)
    def _(c):
        total = conv_chunk(w2b, g2s, 2 * c, 2, width, True)
        delta = s1[:, lanes(2 * c + 5)] * total
        delta = jnp.where(mask[:, lanes(2 * c + 6)] > 0, delta, 0.0).astype(BF)
        spread(g1s, delta.astype(F32), 2 * c * width, width, 1, -1)

    @pl.loop(0, rows // 2)
    def _(c):
        total = conv_chunk(w1b, g1s, 2 * c, 1, width, True)
        base = cot[:, lanes(2 * c + HALO)].astype(F32)
        adj[:, lanes(2 * c)] = (base + total).astype(BF)

    hid = h1.shape[0]

    def nt(a, b):
        return lax.dot_general(a, b, NT, preferred_element_type=F32)

    @pl.loop(0, 3)
    def _(i):
        def window(row):
            return pl.ds(pl.multiple_of(row * width, width), band)

        tl[i] = nt(c3[:, window(3 + (2 - i) * 4)], h2[:, 4 * width : 4 * width + band])
        tf[i] = nt(v3[:, window(6 + i)], g1s[hid : 2 * hid, width : width + band])
        for j in range(3):
            tm[i, j] = nt(
                h1[:, 6 * width : 6 * width + band],
                g2s[j * hid : (j + 1) * hid, window(1 + (2 - i) * 2)],
            )


def early_forward_kernel(rows, width, x, mask, w1, w2, w3, out, v3, h1, h2, s1, s2, h1s, h2s):
    forward_part(rows, width, x, mask, w1, w2, w3, out, v3, h1, h2, s1, s2, h1s, h2s)


def late_kernel(
    rows, width, x, cot, mask, w1, w2, w3, w1b, w2b, w3b, out, adj, tf, tm, tl,
    v3, h1, h2, s1, s2, h1s, h2s, c3, g2s, g1s,
):
    forward_part(rows, width, x, mask, w1, w2, w3, out, v3, h1, h2, s1, s2, h1s, h2s)
    backward_part(rows, width, cot, mask, w1b, w2b, w3b, v3, h1, h2, s1, s2, adj, tf, tm, tl, c3, g2s, g1s)


def early_backward_kernel(
    rows, width, cot, mask, w1b, w2b, w3b, v3, h1, h2, s1, s2, adj, tf, tm, tl, c3, g2s, g1s
):
    backward_part(rows, width, cot, mask, w1b, w2b, w3b, v3, h1, h2, s1, s2, adj, tf, tm, tl, c3, g2s, g1s)


def greet(peers):
    barrier = pltpu.get_barrier_semaphore()
    total = jnp.int32(0)
    for present, peer in peers:
        @pl.when(present)
        def _(peer=peer):
            pl.semaphore_signal(barrier, inc=1, device_id=peer, device_id_type=MESH)

        total = total + present.astype(jnp.int32)
    pl.semaphore_wait(barrier, total)


def halo_kernel(rows, width, lats, state, new, late, early, state_w, new_w, late_w, early_w, low, high, send, recv):
    lat = lax.axis_index("lat")
    step = lax.axis_index("step")
    band, edge = rows * width, HALO * width
    ch = state.shape[0]
    has_low, has_high = lat > 0, lat < lats - 1
    greet([(has_low, {"lat": lat - 1}), (has_high, {"lat": lat + 1})])
    blocks = ((state, state_w), (new, new_w), (late, late_w), (early, early_w))

    def guarded(n, present):
        return (present & (step == 0)) if n == 1 else present

    ups, downs = [], []
    for n, (block, wide) in enumerate(blocks):
        ups.append(pltpu.make_async_remote_copy(
            src_ref=block.at[:, band - edge :], dst_ref=low.at[n], send_sem=send.at[2 * n], recv_sem=recv.at[2 * n],
            device_id={"lat": lat + 1}, device_id_type=MESH,
        ))
        downs.append(pltpu.make_async_remote_copy(
            src_ref=block.at[:, :edge], dst_ref=high.at[n], send_sem=send.at[2 * n + 1],
            recv_sem=recv.at[2 * n + 1], device_id={"lat": lat - 1}, device_id_type=MESH,
        ))
        pl.when(guarded(n, has_high))(ups[n].start)
        pl.when(guarded(n, has_low))(downs[n].start)
    for n, (block, wide) in enumerate(blocks):
        wide[:ch, edge : edge + band] = block[...]
        wide[:ch, :edge] = jnp.zeros((ch, edge), BF)
        wide[:ch, edge + band :] = jnp.zeros((ch, edge), BF)
        wide[ch:, :] = jnp.zeros((wide.shape[0] - ch, band + 2 * edge), BF)
    for n, (block, wide) in enumerate(blocks):
        @pl.when(guarded(n, has_low))
        def _(n=n, wide=wide):
            ups[n].wait_recv()
            wide[:ch, :edge] = low[n]

        @pl.when(guarded(n, has_high))
        def _(n=n, wide=wide):
            downs[n].wait_recv()
            wide[:ch, edge + band :] = high[n]

        pl.when(guarded(n, has_high))(ups[n].wait_send)
        pl.when(guarded(n, has_low))(downs[n].wait_send)


def step_kernel(rows, width, steps, lats, distance, adds, block, base, out, got, send, recv):
    lat = lax.axis_index("lat")
    step = lax.axis_index("step")
    band, edge = rows * width, HALO * width

    def present(s, l):
        return (s >= 0) & (s < steps) & (l >= 0) & (l < lats)

    peers = []
    for s in (step - 1, step + 1):
        for l in (lat - 1, lat, lat + 1):
            peers.append((present(s, l), {"step": s, "lat": l}))
    greet(peers)
    moves = []
    for n, (shift, source, target) in enumerate((
        (1, pl.ds(band - edge, edge), pl.ds(0, edge)),
        (0, pl.ds(0, band), pl.ds(edge, band)),
        (-1, pl.ds(0, edge), pl.ds(edge + band, edge)),
    )):
        copy = pltpu.make_async_remote_copy(
            src_ref=block.at[:, source], dst_ref=got.at[:, target], send_sem=send.at[n], recv_sem=recv.at[n],
            device_id={"step": step + distance, "lat": lat + shift}, device_id_type=MESH,
        )
        pl.when(present(step + distance, lat + shift))(copy.start)
        moves.append((shift, target, copy))
    for shift, target, copy in moves:
        arrives = present(step - distance, lat - shift)

        @pl.when(arrives)
        def _(target=target, copy=copy):
            copy.wait_recv()
            if adds:
                out[:, target] = (base[:, target].astype(F32) + got[:, target].astype(F32)).astype(BF)
            else:
                out[:, target] = got[:, target]

        @pl.when(jnp.logical_not(arrives))
        def _(target=target):
            if adds:
                out[:, target] = base[:, target]
            else:
                first = (step == 0).astype(F32)
                out[:, target] = (base[:, target].astype(F32) * first).astype(BF)

        pl.when(present(step + distance, lat + shift))(copy.wait_send)


def reduce_kernel(
    pairs, lats, piece, scale, *refs
):
    terms, outs = refs[:6], refs[6:9]
    src, got_a, part_b, got_b, part_c, got_c, full, send, recv = refs[9:]
    late_first, late_mid, late_last, early_first, early_mid, early_last = terms
    step = lax.axis_index("step")
    lat = lax.axis_index("lat")
    core = lax.rem(step, 2)
    pair = step // 2
    half, wedge = pairs * lats * piece, lats * piece

    partner = {"step": pair * 2 + (1 - core)}

    def pair_peer(k):
        return {"step": lax.rem(pair + k, pairs) * 2 + core}

    def lat_peer(k):
        return {"lat": lax.rem(lat + k, lats)}

    peers = [partner]
    peers += [pair_peer(k) for k in range(1, pairs)]
    peers += [lat_peer(k) for k in range(1, lats)]
    barrier = pltpu.get_barrier_semaphore()
    for peer in peers:
        pl.semaphore_signal(barrier, inc=1, device_id=peer, device_id_type=MESH)

    cp, hid = late_first.shape[1], late_mid.shape[1]
    lane = src.shape[1]
    rest = hid - lane
    tap_rows = 3 * cp + hid + hid // 2
    taps = late_first.shape[0]

    @pl.loop(0, taps)
    def _(t):
        start = pl.multiple_of(t * tap_rows, 16)
        first = late_first[t] + early_first[t]
        last = late_last[t] + early_last[t]
        mid = late_mid[t] + early_mid[t]
        src[pl.ds(start, cp), :] = first[:, :lane].astype(BF)
        src[pl.ds(start + cp, cp), :] = last[:, :lane].astype(BF)
        src[pl.ds(start + 2 * cp, cp), :] = jnp.concatenate([first[:, lane:], last[:, lane:]], axis=1).astype(BF)
        src[pl.ds(start + 3 * cp, hid), :] = mid[:, :lane].astype(BF)
        src[pl.ds(start + 3 * cp + hid, hid // 2), :] = jnp.concatenate(
            [mid[: hid // 2, lane:], mid[hid // 2 :, lane:]], axis=1
        ).astype(BF)

    used = taps * tap_rows
    if used < src.shape[0]:
        src[used:, :] = jnp.zeros((src.shape[0] - used, lane), BF)
    pl.semaphore_wait(barrier, len(peers))

    count = [0]

    def rows_at(start, size):
        return pl.ds(pl.multiple_of(start, 16), size)

    def copy(source, target, peer):
        slot = count[0]
        count[0] += 1
        made = pltpu.make_async_remote_copy(
            src_ref=source, dst_ref=target, send_sem=send.at[slot], recv_sem=recv.at[slot],
            device_id=peer, device_id_type=MESH,
        )
        made.start()
        return made

    def finish(copies):
        for made in copies:
            made.wait()

    finish([copy(src.at[rows_at((1 - core) * half, half)], got_a, partner)])
    for b in range(pairs):
        mine = src[rows_at(core * half + b * wedge, wedge), :].astype(F32)
        part_b[b * wedge : (b + 1) * wedge, :] = (mine + got_a[b * wedge : (b + 1) * wedge, :].astype(F32)).astype(BF)
    finish([
        copy(part_b.at[rows_at(lax.rem(pair + k, pairs) * wedge, wedge)], got_b.at[k - 1], pair_peer(k))
        for k in range(1, pairs)
    ])
    for c in range(lats):
        total = src[rows_at(core * half + pair * wedge + c * piece, piece), :].astype(F32)
        total = total + got_a[rows_at(pair * wedge + c * piece, piece), :].astype(F32)
        for k in range(pairs - 1):
            total = total + got_b[k, c * piece : (c + 1) * piece, :].astype(F32)
        part_c[c * piece : (c + 1) * piece, :] = total.astype(BF)
    finish([
        copy(part_c.at[rows_at(lax.rem(lat + k, lats) * piece, piece)], got_c.at[k - 1], lat_peer(k))
        for k in range(1, lats)
    ])
    total = part_c[rows_at(lat * piece, piece), :].astype(F32)
    for k in range(lats - 1):
        total = total + got_c[k].astype(F32)
    mine = core * half + pair * wedge + lat * piece
    full[rows_at(mine, piece), :] = (total * scale).astype(BF)
    held = full.at[rows_at(mine, piece)]
    finish([copy(held, held, lat_peer(k)) for k in range(1, lats)])
    held = full.at[rows_at(core * half + pair * wedge, wedge)]
    finish([copy(held, held, pair_peer(k)) for k in range(1, pairs)])
    held = full.at[rows_at(core * half, half)]
    finish([copy(held, held, partner)])

    out_first, out_mid, out_last = outs
    ch = out_first.shape[1]

    @pl.loop(0, taps)
    def _(t):
        start = pl.multiple_of(t * tap_rows, 16)
        tails = full[pl.ds(start + 2 * cp, cp), :].astype(F32)
        out_first[t, :, :lane] = full[pl.ds(start, cp), :].astype(F32)[:ch]
        out_first[t, :, lane:] = tails[:ch, :rest]
        out_last[t, :, :lane] = full[pl.ds(start + cp, cp), :].astype(F32)[:ch]
        out_last[t, :, lane:] = tails[:ch, rest:]
        tails = full[pl.ds(start + 3 * cp + hid, hid // 2), :].astype(F32)
        out_mid[t, :, :lane] = full[pl.ds(start + 3 * cp, hid), :].astype(F32)
        out_mid[t, : hid // 2, lane:] = tails[:, :rest]
        out_mid[t, hid // 2 :, lane:] = tails[:, rest:]


def all_reduce(late_terms, early_terms, ch, scale):
    pairs = lax.axis_size("step") // 2
    lats = lax.axis_size("lat")
    pieces = 2 * pairs * lats
    taps, cp, hid = late_terms[0].shape
    lane = 128
    total = taps * (3 * cp + hid + hid // 2)
    piece = -(-total // (pieces * 16)) * 16
    copies = 2 + 2 * (pairs - 1) + 2 * (lats - 1)
    vmem = pl.BlockSpec(memory_space=pltpu.VMEM)
    return pl.pallas_call(
        functools.partial(reduce_kernel, pairs, lats, piece, scale),
        out_shape=[
            jax.ShapeDtypeStruct((taps, ch, hid), F32),
            jax.ShapeDtypeStruct((taps, hid, hid), F32),
            jax.ShapeDtypeStruct((taps, ch, hid), F32),
        ],
        in_specs=[vmem] * 6,
        out_specs=[vmem] * 3,
        scratch_shapes=[
            pltpu.VMEM((pieces * piece, lane), BF),
            pltpu.VMEM((pairs * lats * piece, lane), BF),
            pltpu.VMEM((pairs * lats * piece, lane), BF),
            pltpu.VMEM((max(pairs - 1, 1), lats * piece, lane), BF),
            pltpu.VMEM((lats * piece, lane), BF),
            pltpu.VMEM((max(lats - 1, 1), piece, lane), BF),
            pltpu.VMEM((pieces * piece, lane), BF),
            pltpu.SemaphoreType.DMA((copies,)),
            pltpu.SemaphoreType.DMA((copies,)),
        ],
        compiler_params=pltpu.CompilerParams(collective_id=0, has_side_effects=True),
        name="kernel_term_sum",
    )(*late_terms, *early_terms)


def body(state_in, new_state, cot_early, cot_late, kernel_first, kernel_mid, kernel_last):
    steps, lats = lax.axis_size("step"), lax.axis_size("lat")
    ch, rows, width = new_state.shape
    hid = kernel_mid.shape[1]
    cp = -(-ch // 16) * 16
    band, edge = rows * width, HALO * width
    lat = lax.axis_index("lat")

    grid_first = jnp.pad(kernel_first.reshape(3, 3, ch, hid), ((0, 0), (0, 0), (0, cp - ch), (0, 0)))
    grid_last = jnp.pad(kernel_last.reshape(3, 3, ch, hid), ((0, 0), (0, 0), (0, cp - ch), (0, 0)))
    grid_mid = kernel_mid.reshape(3, 3, hid, hid)
    w1 = grid_first.transpose(3, 0, 1, 2).reshape(hid, 9 * cp)
    w2 = grid_mid.transpose(3, 0, 1, 2).reshape(hid, 9 * hid)
    w3 = grid_last.transpose(2, 0, 1, 3).reshape(cp, 9 * hid)
    w1b = grid_first.transpose(2, 0, 1, 3).reshape(cp, 9 * hid)
    w2b = grid_mid.transpose(2, 0, 1, 3).reshape(hid, 9 * hid)
    w3b = grid_last.transpose(3, 0, 1, 2).reshape(hid, 9 * cp)

    ext_row = lat * rows + jnp.arange(rows + 2 * HALO, dtype=jnp.int32) - HALO
    inside = (ext_row >= 0) & (ext_row < rows * lats)
    mask = jnp.repeat(inside.astype(F32), width)[None]

    vmem_spec = pl.BlockSpec(memory_space=pltpu.VMEM)
    wide_shape = jax.ShapeDtypeStruct((cp, band + 2 * edge), BF)
    state_w, new_w, late_cot_w, early_cot_w = pl.pallas_call(
        functools.partial(halo_kernel, rows, width, lats),
        out_shape=[wide_shape] * 4,
        in_specs=[vmem_spec] * 4,
        out_specs=[vmem_spec] * 4,
        scratch_shapes=[
            pltpu.VMEM((4, ch, edge), BF), pltpu.VMEM((4, ch, edge), BF),
            pltpu.SemaphoreType.DMA((8,)), pltpu.SemaphoreType.DMA((8,)),
        ],
        compiler_params=pltpu.CompilerParams(collective_id=1, has_side_effects=True),
        name="halos",
    )(*(block.reshape(ch, band) for block in (state_in[0], new_state, cot_late[0], cot_early[0])))

    def to_step(block, base, distance, adds):
        return pl.pallas_call(
            functools.partial(step_kernel, rows, width, steps, lats, distance, adds),
            out_shape=wide_shape,
            in_specs=[vmem_spec] * 2,
            out_specs=vmem_spec,
            scratch_shapes=[
                pltpu.VMEM(wide_shape.shape, BF),
                pltpu.SemaphoreType.DMA((3,)), pltpu.SemaphoreType.DMA((3,)),
            ],
            compiler_params=pltpu.CompilerParams(collective_id=3 if adds else 2, has_side_effects=True),
            name="step_cotangent" if adds else "step_state",
        )(block, base)

    vmem = pl.BlockSpec(memory_space=pltpu.VMEM)
    shape = jax.ShapeDtypeStruct
    lanes_v, lanes_1, lanes_2 = (rows + 14) * width, (rows + 12) * width, (rows + 8) * width
    saved_shapes = [
        ((3 * cp, lanes_v), BF), ((hid, lanes_1), BF), ((hid, lanes_2), BF),
        ((hid, lanes_1), F32), ((hid, lanes_2), F32),
    ]
    fwd_scratch = [((3 * hid, lanes_1), BF), ((3 * hid, lanes_2), BF)]
    bwd_scratch = [
        ((3 * cp, lanes_v), BF), ((3 * hid, (rows + 6) * width), BF), ((3 * hid, (rows + 2) * width), BF)
    ]
    bwd_outs = [
        ((cp, band), BF), ((3, 3 * cp, hid), F32), ((3, 3, hid, hid), F32), ((3, 3 * cp, hid), F32)
    ]

    def call(kernel, name, ins, outs, scratch):
        return pl.pallas_call(
            functools.partial(kernel, rows, width),
            out_shape=[shape(*o) for o in outs],
            in_specs=[vmem] * len(ins),
            out_specs=[vmem] * len(outs),
            scratch_shapes=[pltpu.VMEM(*s) for s in scratch],
            compiler_params=pltpu.CompilerParams(vmem_limit_bytes=56 * 1024 * 1024),
            name=name,
        )(*ins)

    early_out, *saved = call(
        early_forward_kernel, "early_forward", (state_w, mask, w1, w2, w3),
        [((cp, band), BF)] + saved_shapes, fwd_scratch,
    )
    late_in = to_step(early_out, new_w, 1, False)
    late_out, late_adj, *late_terms = call(
        late_kernel, "late_both", (late_in, late_cot_w, mask, w1, w2, w3, w1b, w2b, w3b),
        [((cp, band), BF)] + bwd_outs, saved_shapes + fwd_scratch + bwd_scratch,
    )
    early_cot = to_step(late_adj, early_cot_w, -1, True)
    state_adj, *early_terms = call(
        early_backward_kernel, "early_backward", (early_cot, mask, w1b, w2b, w3b, *saved),
        bwd_outs, bwd_scratch,
    )

    def by_tap(terms):
        first, mid, last = terms
        return first.reshape(9, cp, hid), mid.reshape(9, hid, hid), last.reshape(9, cp, hid)

    scale = 1.0 / math.sqrt(2.0 * steps * rows * lats * width)
    first, mid, last = all_reduce(by_tap(late_terms), by_tap(early_terms), ch, scale)
    return (
        late_out[:ch].reshape(1, ch, rows, width),
        state_adj[:ch].reshape(1, ch, rows, width),
        first,
        mid,
        last,
    )


def solution(mesh):
    banded = P("step", None, "lat", None)
    return jax.shard_map(
        body,
        mesh=mesh,
        in_specs=(banded, P(None, "lat", None), banded, banded, P(), P(), P()),
        out_specs=(banded, banded, P(), P(), P()),
        check_vma=False,
    )
```

```python
import functools
import math

import jax
import jax.numpy as jnp
from jax import lax
from jax.experimental import pallas as pl
from jax.experimental.pallas import tpu as pltpu
from jax.sharding import PartitionSpec as P

MESH = pl.DeviceIdType.MESH
BF = jnp.bfloat16
F32 = jnp.float32
HALO = 7
NT = (((1,), (1,)), ((), ()))


def gelu_pair(a):
    k = math.sqrt(2.0 / math.pi)
    sq = a * a
    t = jnp.tanh(k * (a + 0.044715 * (sq * a)))
    half = 0.5 * (1.0 + t)
    slope = half + (0.5 * a) * (1.0 - t * t) * (k * (1.0 + (3.0 * 0.044715) * sq))
    return a * half, slope


def spread(dst, value, lane, width, dilation, sign):
    channels = value.shape[0]
    column = lax.broadcasted_iota(jnp.int32, (channels, width), 1)
    for k in range(value.shape[1] // width):
        piece = value[:, k * width : (k + 1) * width]
        for j in range(3):
            shift = sign * dilation * (j - 1)
            if shift == 0:
                moved = piece
            else:
                moved = pltpu.roll(piece, (-shift) % width, 1)
                good = (column + shift >= 0) & (column + shift < width)
                moved = jnp.where(good, moved, 0.0)
            dst[j * channels : (j + 1) * channels, pl.ds(pl.multiple_of(lane + k * width, width), width)] = (
                moved.astype(BF)
            )


def conv_chunk(weights, src, row, dilation, width, back, first_row=0):
    windows = []
    for i in range(3):
        offset = (2 - i if back else i) * dilation + first_row
        lane = pl.multiple_of((row + offset) * width, width)
        windows.append(src[:, pl.ds(lane, 2 * width)])
    return jnp.dot(weights[...], jnp.concatenate(windows, axis=0), preferred_element_type=F32)


def forward_part(rows, width, x, mask, w1, w2, w3, out, v3, h1, h2, s1, s2, h1s, h2s):
    chunk = 2 * width
    hid = s1.shape[0]

    def lanes(row):
        return pl.ds(pl.multiple_of(row * width, width), chunk)

    @pl.loop(0, (rows + 14) // 2)
    def _(c):
        spread(v3, x[:, lanes(2 * c)].astype(F32), 2 * c * width, width, 1, 1)

    @pl.loop(0, (rows + 12) // 2, unroll=2)
    def _(c):
        value, slope = gelu_pair(conv_chunk(w1, v3, 2 * c, 1, width, False))
        value = jnp.where(mask[:, lanes(2 * c + 1)] > 0, value, 0.0).astype(BF)
        s1[:, lanes(2 * c)] = slope.astype(BF)
        spread(h1s, value.astype(F32), 2 * c * width, width, 2, 1)

    @pl.loop(0, (rows + 8) // 2, unroll=2)
    def _(c):
        value, slope = gelu_pair(conv_chunk(w2, h1s, 2 * c, 2, width, False))
        value = jnp.where(mask[:, lanes(2 * c + 3)] > 0, value, 0.0).astype(BF)
        s2[:, lanes(2 * c)] = slope.astype(BF)
        spread(h2s, value.astype(F32), 2 * c * width, width, 4, 1)

    @pl.loop(0, rows // 2, unroll=2)
    def _(c):
        total = conv_chunk(w3, h2s, 2 * c, 4, width, False)
        base = x[:, lanes(2 * c + HALO)].astype(F32)
        out[:, lanes(2 * c)] = (base + total).astype(BF)
        if h1 is not None:
            h1[:, lanes(2 * c)] = h1s[hid : 2 * hid, lanes(2 * c + 6)]
            h2[:, lanes(2 * c)] = h2s[hid : 2 * hid, lanes(2 * c + 4)]


def backward_part(rows, width, cot, mask, w1b, w2b, w3b, v3, h1, h2, s1, s2, adj, tf, tm, tl, c3, g2s, g1s):
    chunk = 2 * width
    band = rows * width

    def lanes(row):
        return pl.ds(pl.multiple_of(row * width, width), chunk)

    @pl.loop(0, (rows + 14) // 2)
    def _(c):
        spread(c3, cot[:, lanes(2 * c)].astype(F32), 2 * c * width, width, 4, -1)

    @pl.loop(0, (rows + 6) // 2)
    def _(c):
        total = conv_chunk(w3b, c3, 2 * c, 4, width, True)
        delta = s2[:, lanes(2 * c + 1)].astype(F32) * total
        delta = jnp.where(mask[:, lanes(2 * c + 4)] > 0, delta, 0.0).astype(BF)
        spread(g2s, delta.astype(F32), 2 * c * width, width, 2, -1)

    @pl.loop(0, (rows + 2) // 2)
    def _(c):
        total = conv_chunk(w2b, g2s, 2 * c, 2, width, True)
        delta = s1[:, lanes(2 * c + 5)].astype(F32) * total
        delta = jnp.where(mask[:, lanes(2 * c + 6)] > 0, delta, 0.0).astype(BF)
        spread(g1s, delta.astype(F32), 2 * c * width, width, 1, -1)

    @pl.loop(0, rows // 2, unroll=2)
    def _(c):
        total = conv_chunk(w1b, g1s, 2 * c, 1, width, True)
        base = cot[:, lanes(2 * c + HALO)].astype(F32)
        adj[:, lanes(2 * c)] = (base + total).astype(BF)

    hid = h1.shape[0]

    def nt(a, b):
        return lax.dot_general(a, b, NT, preferred_element_type=F32)

    @pl.loop(0, 3)
    def _(i):
        def window(row):
            return pl.ds(pl.multiple_of(row * width, width), band)

        tl[i] = nt(c3[:, window(3 + (2 - i) * 4)], h2[...])
        tf[i] = nt(v3[:, window(6 + i)], g1s[hid : 2 * hid, width : width + band])
        for j in range(3):
            tm[i, j] = nt(
                h1[...],
                g2s[j * hid : (j + 1) * hid, window(1 + (2 - i) * 2)],
            )


def early_forward_kernel(rows, width, x, mask, w1, w2, w3, out, v3, h1, h2, s1, s2, h1s, h2s):
    forward_part(rows, width, x, mask, w1, w2, w3, out, v3, h1, h2, s1, s2, h1s, h2s)


def late_kernel(
    rows, width, x, cot, mask, w1, w2, w3, w1b, w2b, w3b, out, adj, tf, tm, tl,
    v3, s1, s2, h1s, h2s, c3, g2s, g1s,
):
    forward_part(rows, width, x, mask, w1, w2, w3, out, v3, None, None, s1, s2, h1s, h2s)
    hid, band = s1.shape[0], rows * width
    h1 = h1s.at[hid : 2 * hid, 6 * width : 6 * width + band]
    h2 = h2s.at[hid : 2 * hid, 4 * width : 4 * width + band]
    backward_part(rows, width, cot, mask, w1b, w2b, w3b, v3, h1, h2, s1, s2, adj, tf, tm, tl, c3, g2s, g1s)


def early_backward_kernel(
    rows, width, cot, mask, w1b, w2b, w3b, v3, h1, h2, s1, s2, adj, tf, tm, tl, c3, g2s, g1s
):
    backward_part(rows, width, cot, mask, w1b, w2b, w3b, v3, h1, h2, s1, s2, adj, tf, tm, tl, c3, g2s, g1s)


def greet(peers):
    barrier = pltpu.get_barrier_semaphore()
    total = jnp.int32(0)
    for present, peer in peers:
        @pl.when(present)
        def _(peer=peer):
            pl.semaphore_signal(barrier, inc=1, device_id=peer, device_id_type=MESH)

        total = total + present.astype(jnp.int32)
    pl.semaphore_wait(barrier, total)


def halo_kernel(rows, width, lats, state, new, late, early, state_w, new_w, late_w, early_w, low, high, send, recv):
    lat = lax.axis_index("lat")
    step = lax.axis_index("step")
    band, edge = rows * width, HALO * width
    ch = state.shape[0]
    has_low, has_high = lat > 0, lat < lats - 1
    greet([(has_low, {"lat": lat - 1}), (has_high, {"lat": lat + 1})])
    blocks = ((state, state_w), (new, new_w), (late, late_w), (early, early_w))

    def guarded(n, present):
        return (present & (step == 0)) if n == 1 else present

    ups, downs = [], []
    for n, (block, wide) in enumerate(blocks):
        ups.append(pltpu.make_async_remote_copy(
            src_ref=block.at[:, band - edge :], dst_ref=low.at[n], send_sem=send.at[2 * n], recv_sem=recv.at[2 * n],
            device_id={"lat": lat + 1}, device_id_type=MESH,
        ))
        downs.append(pltpu.make_async_remote_copy(
            src_ref=block.at[:, :edge], dst_ref=high.at[n], send_sem=send.at[2 * n + 1],
            recv_sem=recv.at[2 * n + 1], device_id={"lat": lat - 1}, device_id_type=MESH,
        ))
        pl.when(guarded(n, has_high))(ups[n].start)
        pl.when(guarded(n, has_low))(downs[n].start)
    for n, (block, wide) in enumerate(blocks):
        wide[:ch, edge : edge + band] = block[...]
        wide[:ch, :edge] = jnp.zeros((ch, edge), BF)
        wide[:ch, edge + band :] = jnp.zeros((ch, edge), BF)
        wide[ch:, :] = jnp.zeros((wide.shape[0] - ch, band + 2 * edge), BF)
    for n, (block, wide) in enumerate(blocks):
        @pl.when(guarded(n, has_low))
        def _(n=n, wide=wide):
            ups[n].wait_recv()
            wide[:ch, :edge] = low[n]

        @pl.when(guarded(n, has_high))
        def _(n=n, wide=wide):
            downs[n].wait_recv()
            wide[:ch, edge + band :] = high[n]

        pl.when(guarded(n, has_high))(ups[n].wait_send)
        pl.when(guarded(n, has_low))(downs[n].wait_send)


def step_kernel(rows, width, steps, lats, distance, adds, block, base, out, got, send, recv):
    lat = lax.axis_index("lat")
    step = lax.axis_index("step")
    band, edge = rows * width, HALO * width

    def present(s, l):
        return (s >= 0) & (s < steps) & (l >= 0) & (l < lats)

    peers = []
    for s in (step - 1, step + 1):
        for l in (lat - 1, lat, lat + 1):
            peers.append((present(s, l), {"step": s, "lat": l}))
    greet(peers)
    moves = []
    for n, (shift, source, target) in enumerate((
        (1, pl.ds(band - edge, edge), pl.ds(0, edge)),
        (0, pl.ds(0, band), pl.ds(edge, band)),
        (-1, pl.ds(0, edge), pl.ds(edge + band, edge)),
    )):
        copy = pltpu.make_async_remote_copy(
            src_ref=block.at[:, source], dst_ref=got.at[:, target], send_sem=send.at[n], recv_sem=recv.at[n],
            device_id={"step": step + distance, "lat": lat + shift}, device_id_type=MESH,
        )
        pl.when(present(step + distance, lat + shift))(copy.start)
        moves.append((shift, target, copy))
    for shift, target, copy in moves:
        arrives = present(step - distance, lat - shift)

        @pl.when(arrives)
        def _(target=target, copy=copy):
            copy.wait_recv()
            if adds:
                out[:, target] = (base[:, target].astype(F32) + got[:, target].astype(F32)).astype(BF)
            else:
                out[:, target] = got[:, target]

        @pl.when(jnp.logical_not(arrives))
        def _(target=target):
            if adds:
                out[:, target] = base[:, target]
            else:
                first = (step == 0).astype(F32)
                out[:, target] = (base[:, target].astype(F32) * first).astype(BF)

        pl.when(present(step + distance, lat + shift))(copy.wait_send)


def reduce_kernel(
    pairs, lats, piece, scale, *refs
):
    terms, out = refs[:6], refs[6]
    src, got_a, part_b, got_b, part_c, got_c, full, send, recv = refs[7:]
    late_first, late_mid, late_last, early_first, early_mid, early_last = terms
    step = lax.axis_index("step")
    lat = lax.axis_index("lat")
    core = lax.rem(step, 2)
    pair = step // 2
    half, wedge = pairs * lats * piece, lats * piece
    segments = got_a.shape[0]

    partner = {"step": pair * 2 + (1 - core)}

    def pair_peer(k):
        return {"step": lax.rem(pair + k, pairs) * 2 + core}

    def lat_peer(k):
        return {"lat": lax.rem(lat + k, lats)}

    peers = [partner]
    peers += [pair_peer(k) for k in range(1, pairs)]
    peers += [lat_peer(k) for k in range(1, lats)]
    barrier = pltpu.get_barrier_semaphore()
    for peer in peers:
        pl.semaphore_signal(barrier, inc=1, device_id=peer, device_id_type=MESH)

    cp, hid = late_first.shape[1], late_mid.shape[1]
    lane = src.shape[1]
    rest = hid - lane
    tap_rows = 3 * cp + hid + hid // 2
    taps = late_first.shape[0]

    @pl.loop(0, taps)
    def _(t):
        start = pl.multiple_of(t * tap_rows, 16)
        first = late_first[t] + early_first[t]
        last = late_last[t] + early_last[t]
        mid = late_mid[t] + early_mid[t]
        src[pl.ds(start, cp), :] = first[:, :lane].astype(BF)
        src[pl.ds(start + cp, cp), :] = last[:, :lane].astype(BF)
        src[pl.ds(start + 2 * cp, cp), :] = jnp.concatenate([first[:, lane:], last[:, lane:]], axis=1).astype(BF)
        src[pl.ds(start + 3 * cp, hid), :] = mid[:, :lane].astype(BF)
        src[pl.ds(start + 3 * cp + hid, hid // 2), :] = jnp.concatenate(
            [mid[: hid // 2, lane:], mid[hid // 2 :, lane:]], axis=1
        ).astype(BF)

    used = taps * tap_rows
    if used < src.shape[0]:
        src[used:, :] = jnp.zeros((src.shape[0] - used, lane), BF)
    pl.semaphore_wait(barrier, len(peers))

    count = [0]

    def rows_at(start, size):
        return pl.ds(pl.multiple_of(start, 16), size)

    def copy(source, target, peer):
        slot = count[0]
        count[0] += 1
        made = pltpu.make_async_remote_copy(
            src_ref=source, dst_ref=target, send_sem=send.at[slot], recv_sem=recv.at[slot],
            device_id=peer, device_id_type=MESH,
        )
        made.start()
        return made

    def finish(copies):
        for made in copies:
            made.wait()

    def stage_b(q):
        base = q * 2 * half + core * half
        for b in range(pairs):
            mine = src[rows_at(base + b * wedge, wedge), :].astype(F32)
            theirs = got_a[q, b * wedge : (b + 1) * wedge, :].astype(F32)
            part_b[q, b * wedge : (b + 1) * wedge, :] = (mine + theirs).astype(BF)
        return [
            copy(part_b.at[q, rows_at(lax.rem(pair + k, pairs) * wedge, wedge)], got_b.at[q, k - 1], pair_peer(k))
            for k in range(1, pairs)
        ]

    def stage_c(q):
        base = q * 2 * half + core * half + pair * wedge
        for c in range(lats):
            total = src[rows_at(base + c * piece, piece), :].astype(F32)
            total = total + got_a[q, rows_at(pair * wedge + c * piece, piece), :].astype(F32)
            for k in range(pairs - 1):
                total = total + got_b[q, k, c * piece : (c + 1) * piece, :].astype(F32)
            part_c[q, c * piece : (c + 1) * piece, :] = total.astype(BF)
        return [
            copy(part_c.at[q, rows_at(lax.rem(lat + k, lats) * piece, piece)], got_c.at[q, k - 1], lat_peer(k))
            for k in range(1, lats)
        ]

    def spread_c(q):
        total = part_c[q, rows_at(lat * piece, piece), :].astype(F32)
        for k in range(lats - 1):
            total = total + got_c[q, k].astype(F32)
        mine = rows_at(q * 2 * half + core * half + pair * wedge + lat * piece, piece)
        full[mine, :] = (total * scale).astype(BF)
        return [copy(full.at[mine], full.at[mine], lat_peer(k)) for k in range(1, lats)]

    def spread_b(q):
        held = full.at[rows_at(q * 2 * half + core * half + pair * wedge, wedge)]
        return [copy(held, held, pair_peer(k)) for k in range(1, pairs)]

    def spread_a(q):
        held = full.at[rows_at(q * 2 * half + core * half, half)]
        return [copy(held, held, partner)]

    flying = [
        [copy(src.at[rows_at(q * 2 * half + (1 - core) * half, half)], got_a.at[q], partner)]
        for q in range(segments)
    ]
    for stage in (stage_b, stage_c, spread_c, spread_b, spread_a):
        for q in range(segments):
            finish(flying[q])
            flying[q] = stage(q)
    for q in range(segments):
        finish(flying[q])
    out[...] = full[...]


def unpack_kernel(packed, out_first, out_mid, out_last):
    ch, hid = out_first.shape[1:]
    lane = packed.shape[1]
    rest = hid - lane
    cp = (packed.shape[0] - hid - hid // 2) // 3
    tails = packed[2 * cp : 3 * cp, :].astype(F32)
    out_first[0, :, :lane] = packed[:cp, :].astype(F32)[:ch]
    out_first[0, :, lane:] = tails[:ch, :rest]
    out_last[0, :, :lane] = packed[cp : 2 * cp, :].astype(F32)[:ch]
    out_last[0, :, lane:] = tails[:ch, rest:]
    tails = packed[3 * cp + hid :, :].astype(F32)
    out_mid[0, :, :lane] = packed[3 * cp : 3 * cp + hid, :].astype(F32)
    out_mid[0, : hid // 2, lane:] = tails[:, :rest]
    out_mid[0, hid // 2 :, lane:] = tails[:, rest:]


def all_reduce(late_terms, early_terms, ch, scale):
    pairs = lax.axis_size("step") // 2
    lats = lax.axis_size("lat")
    pieces = 2 * pairs * lats
    taps, cp, hid = late_terms[0].shape
    lane = 128
    tap_rows = 3 * cp + hid + hid // 2
    segments = 2
    piece = -(-taps * tap_rows // (segments * pieces * 16)) * 16
    rows = segments * pieces * piece
    copies = segments * (2 + 2 * (pairs - 1) + 2 * (lats - 1))
    vmem = pl.BlockSpec(memory_space=pltpu.VMEM)
    packed = pl.pallas_call(
        functools.partial(reduce_kernel, pairs, lats, piece, scale),
        out_shape=jax.ShapeDtypeStruct((rows, lane), BF),
        in_specs=[vmem] * 6,
        out_specs=vmem,
        scratch_shapes=[
            pltpu.VMEM((rows, lane), BF),
            pltpu.VMEM((segments, pairs * lats * piece, lane), BF),
            pltpu.VMEM((segments, pairs * lats * piece, lane), BF),
            pltpu.VMEM((segments, max(pairs - 1, 1), lats * piece, lane), BF),
            pltpu.VMEM((segments, lats * piece, lane), BF),
            pltpu.VMEM((segments, max(lats - 1, 1), piece, lane), BF),
            pltpu.VMEM((rows, lane), BF),
            pltpu.SemaphoreType.DMA((copies,)),
            pltpu.SemaphoreType.DMA((copies,)),
        ],
        compiler_params=pltpu.CompilerParams(collective_id=0, has_side_effects=True),
        name="kernel_term_sum",
    )(*late_terms, *early_terms)
    return pl.pallas_call(
        unpack_kernel,
        grid=(taps,),
        out_shape=[
            jax.ShapeDtypeStruct((taps, ch, hid), F32),
            jax.ShapeDtypeStruct((taps, hid, hid), F32),
            jax.ShapeDtypeStruct((taps, ch, hid), F32),
        ],
        in_specs=[pl.BlockSpec((tap_rows, lane), lambda t: (t, 0))],
        out_specs=[
            pl.BlockSpec((1, ch, hid), lambda t: (t, 0, 0)),
            pl.BlockSpec((1, hid, hid), lambda t: (t, 0, 0)),
            pl.BlockSpec((1, ch, hid), lambda t: (t, 0, 0)),
        ],
        name="unpack_terms",
    )(packed)


def body(state_in, new_state, cot_early, cot_late, kernel_first, kernel_mid, kernel_last):
    steps, lats = lax.axis_size("step"), lax.axis_size("lat")
    ch, rows, width = new_state.shape
    hid = kernel_mid.shape[1]
    cp = -(-ch // 16) * 16
    band, edge = rows * width, HALO * width
    lat = lax.axis_index("lat")

    grid_first = jnp.pad(kernel_first.reshape(3, 3, ch, hid), ((0, 0), (0, 0), (0, cp - ch), (0, 0)))
    grid_last = jnp.pad(kernel_last.reshape(3, 3, ch, hid), ((0, 0), (0, 0), (0, cp - ch), (0, 0)))
    grid_mid = kernel_mid.reshape(3, 3, hid, hid)
    w1 = grid_first.transpose(3, 0, 1, 2).reshape(hid, 9 * cp)
    w2 = grid_mid.transpose(3, 0, 1, 2).reshape(hid, 9 * hid)
    w3 = grid_last.transpose(2, 0, 1, 3).reshape(cp, 9 * hid)
    w1b = grid_first.transpose(2, 0, 1, 3).reshape(cp, 9 * hid)
    w2b = grid_mid.transpose(2, 0, 1, 3).reshape(hid, 9 * hid)
    w3b = grid_last.transpose(3, 0, 1, 2).reshape(hid, 9 * cp)

    ext_row = lat * rows + jnp.arange(rows + 2 * HALO, dtype=jnp.int32) - HALO
    inside = (ext_row >= 0) & (ext_row < rows * lats)
    mask = jnp.repeat(inside.astype(F32), width)[None]

    vmem_spec = pl.BlockSpec(memory_space=pltpu.VMEM)
    wide_shape = jax.ShapeDtypeStruct((cp, band + 2 * edge), BF)
    state_w, new_w, late_cot_w, early_cot_w = pl.pallas_call(
        functools.partial(halo_kernel, rows, width, lats),
        out_shape=[wide_shape] * 4,
        in_specs=[vmem_spec] * 4,
        out_specs=[vmem_spec] * 4,
        scratch_shapes=[
            pltpu.VMEM((4, ch, edge), BF), pltpu.VMEM((4, ch, edge), BF),
            pltpu.SemaphoreType.DMA((8,)), pltpu.SemaphoreType.DMA((8,)),
        ],
        compiler_params=pltpu.CompilerParams(collective_id=1, has_side_effects=True),
        name="halos",
    )(*(block.reshape(ch, band) for block in (state_in[0], new_state, cot_late[0], cot_early[0])))

    def to_step(block, base, distance, adds):
        return pl.pallas_call(
            functools.partial(step_kernel, rows, width, steps, lats, distance, adds),
            out_shape=wide_shape,
            in_specs=[vmem_spec] * 2,
            out_specs=vmem_spec,
            scratch_shapes=[
                pltpu.VMEM(wide_shape.shape, BF),
                pltpu.SemaphoreType.DMA((3,)), pltpu.SemaphoreType.DMA((3,)),
            ],
            compiler_params=pltpu.CompilerParams(collective_id=3 if adds else 2, has_side_effects=True),
            name="step_cotangent" if adds else "step_state",
        )(block, base)

    vmem = pl.BlockSpec(memory_space=pltpu.VMEM)
    shape = jax.ShapeDtypeStruct
    lanes_v, lanes_1, lanes_2 = (rows + 14) * width, (rows + 12) * width, (rows + 8) * width
    saved_shapes = [
        ((3 * cp, lanes_v), BF), ((hid, band), BF), ((hid, band), BF),
        ((hid, lanes_1), BF), ((hid, lanes_2), BF),
    ]
    fwd_scratch = [((3 * hid, lanes_1), BF), ((3 * hid, lanes_2), BF)]
    bwd_scratch = [
        ((3 * cp, lanes_v), BF), ((3 * hid, (rows + 6) * width), BF), ((3 * hid, (rows + 2) * width), BF)
    ]
    bwd_outs = [
        ((cp, band), BF), ((3, 3 * cp, hid), F32), ((3, 3, hid, hid), F32), ((3, 3 * cp, hid), F32)
    ]

    def call(kernel, name, ins, outs, scratch):
        return pl.pallas_call(
            functools.partial(kernel, rows, width),
            out_shape=[shape(*o) for o in outs],
            in_specs=[vmem] * len(ins),
            out_specs=[vmem] * len(outs),
            scratch_shapes=[pltpu.VMEM(*s) for s in scratch],
            compiler_params=pltpu.CompilerParams(vmem_limit_bytes=56 * 1024 * 1024),
            name=name,
        )(*ins)

    early_out, *saved = call(
        early_forward_kernel, "early_forward", (state_w, mask, w1, w2, w3),
        [((cp, band), BF)] + saved_shapes, fwd_scratch,
    )
    late_in = to_step(early_out, new_w, 1, False)
    late_out, late_adj, *late_terms = call(
        late_kernel, "late_both", (late_in, late_cot_w, mask, w1, w2, w3, w1b, w2b, w3b),
        [((cp, band), BF)] + bwd_outs, saved_shapes[:1] + saved_shapes[3:] + fwd_scratch + bwd_scratch,
    )
    early_cot = to_step(late_adj, early_cot_w, -1, True)
    state_adj, *early_terms = call(
        early_backward_kernel, "early_backward", (early_cot, mask, w1b, w2b, w3b, *saved),
        bwd_outs, bwd_scratch,
    )

    def by_tap(terms):
        first, mid, last = terms
        return first.reshape(9, cp, hid), mid.reshape(9, hid, hid), last.reshape(9, cp, hid)

    scale = 1.0 / math.sqrt(2.0 * steps * rows * lats * width)
    first, mid, last = all_reduce(by_tap(late_terms), by_tap(early_terms), ch, scale)
    return (
        late_out[:ch].reshape(1, ch, rows, width),
        state_adj[:ch].reshape(1, ch, rows, width),
        first,
        mid,
        last,
    )


def solution(mesh):
    banded = P("step", None, "lat", None)
    return jax.shard_map(
        body,
        mesh=mesh,
        in_specs=(banded, P(None, "lat", None), banded, banded, P(), P(), P()),
        out_specs=(banded, banded, P(), P(), P()),
        check_vma=False,
    )
```

```python
import functools
import math

import jax
import jax.numpy as jnp
from jax import lax
from jax.experimental import pallas as pl
from jax.experimental.pallas import tpu as pltpu
from jax.sharding import PartitionSpec as P

MESH = pl.DeviceIdType.MESH
BF = jnp.bfloat16
F32 = jnp.float32
HALO = 7
NT = (((1,), (1,)), ((), ()))


def gelu_pair(a):
    k = math.sqrt(2.0 / math.pi)
    sq = a * a
    t = jnp.tanh(k * (a + 0.044715 * (sq * a)))
    half = 0.5 * (1.0 + t)
    slope = half + (0.5 * a) * (1.0 - t * t) * (k * (1.0 + (3.0 * 0.044715) * sq))
    return a * half, slope


def spread(dst, value, lane, width, dilation, sign):
    channels = value.shape[0]
    column = lax.broadcasted_iota(jnp.int32, (channels, width), 1)
    for k in range(value.shape[1] // width):
        piece = value[:, k * width : (k + 1) * width]
        for j in range(3):
            shift = sign * dilation * (j - 1)
            if shift == 0:
                moved = piece
            else:
                moved = pltpu.roll(piece, (-shift) % width, 1)
                good = (column + shift >= 0) & (column + shift < width)
                moved = jnp.where(good, moved, 0.0)
            dst[j * channels : (j + 1) * channels, pl.ds(pl.multiple_of(lane + k * width, width), width)] = (
                moved.astype(BF)
            )


def conv_chunk(weights, src, row, dilation, width, back, first_row=0):
    windows = []
    for i in range(3):
        offset = (2 - i if back else i) * dilation + first_row
        lane = pl.multiple_of((row + offset) * width, width)
        windows.append(src[:, pl.ds(lane, 2 * width)])
    return jnp.dot(weights[...], jnp.concatenate(windows, axis=0), preferred_element_type=F32)


def forward_part(rows, width, x, mask, w1, w2, w3, out, v3, h1, h2, s1, s2, h1s, h2s):
    chunk = 2 * width
    hid = s1.shape[0]

    def lanes(row):
        return pl.ds(pl.multiple_of(row * width, width), chunk)

    @pl.loop(0, (rows + 14) // 2)
    def _(c):
        spread(v3, x[:, lanes(2 * c)].astype(F32), 2 * c * width, width, 1, 1)

    @pl.loop(0, (rows + 12) // 2, unroll=2)
    def _(c):
        value, slope = gelu_pair(conv_chunk(w1, v3, 2 * c, 1, width, False))
        value = jnp.where(mask[:, lanes(2 * c + 1)] > 0, value, 0.0).astype(BF)
        s1[:, lanes(2 * c)] = slope.astype(BF)
        spread(h1s, value.astype(F32), 2 * c * width, width, 2, 1)

    @pl.loop(0, (rows + 8) // 2, unroll=2)
    def _(c):
        value, slope = gelu_pair(conv_chunk(w2, h1s, 2 * c, 2, width, False))
        value = jnp.where(mask[:, lanes(2 * c + 3)] > 0, value, 0.0).astype(BF)
        s2[:, lanes(2 * c)] = slope.astype(BF)
        spread(h2s, value.astype(F32), 2 * c * width, width, 4, 1)

    @pl.loop(0, rows // 2, unroll=2)
    def _(c):
        total = conv_chunk(w3, h2s, 2 * c, 4, width, False)
        base = x[:, lanes(2 * c + HALO)].astype(F32)
        out[:, lanes(2 * c)] = (base + total).astype(BF)
        if h1 is not None:
            h1[:, lanes(2 * c)] = h1s[hid : 2 * hid, lanes(2 * c + 6)]
            h2[:, lanes(2 * c)] = h2s[hid : 2 * hid, lanes(2 * c + 4)]


def backward_part(rows, width, cot, mask, w1b, w2b, w3b, v3, h1, h2, s1, s2, adj, tf, tm, tl, c3, g2s, g1s):
    chunk = 2 * width
    band = rows * width

    def lanes(row):
        return pl.ds(pl.multiple_of(row * width, width), chunk)

    @pl.loop(0, (rows + 14) // 2)
    def _(c):
        spread(c3, cot[:, lanes(2 * c)].astype(F32), 2 * c * width, width, 4, -1)

    @pl.loop(0, (rows + 6) // 2)
    def _(c):
        total = conv_chunk(w3b, c3, 2 * c, 4, width, True)
        delta = s2[:, lanes(2 * c + 1)].astype(F32) * total
        delta = jnp.where(mask[:, lanes(2 * c + 4)] > 0, delta, 0.0).astype(BF)
        spread(g2s, delta.astype(F32), 2 * c * width, width, 2, -1)

    @pl.loop(0, (rows + 2) // 2)
    def _(c):
        total = conv_chunk(w2b, g2s, 2 * c, 2, width, True)
        delta = s1[:, lanes(2 * c + 5)].astype(F32) * total
        delta = jnp.where(mask[:, lanes(2 * c + 6)] > 0, delta, 0.0).astype(BF)
        spread(g1s, delta.astype(F32), 2 * c * width, width, 1, -1)

    @pl.loop(0, rows // 2, unroll=2)
    def _(c):
        total = conv_chunk(w1b, g1s, 2 * c, 1, width, True)
        base = cot[:, lanes(2 * c + HALO)].astype(F32)
        adj[:, lanes(2 * c)] = (base + total).astype(BF)

    hid = h1.shape[0]

    def nt(a, b):
        return lax.dot_general(a, b, NT, preferred_element_type=F32)

    @pl.loop(0, 3)
    def _(i):
        def window(row):
            return pl.ds(pl.multiple_of(row * width, width), band)

        tl[i] = nt(c3[:, window(3 + (2 - i) * 4)], h2[...])
        tf[i] = nt(v3[:, window(6 + i)], g1s[hid : 2 * hid, width : width + band])
        for j in range(3):
            tm[i, j] = nt(
                h1[...],
                g2s[j * hid : (j + 1) * hid, window(1 + (2 - i) * 2)],
            )


def early_forward_kernel(rows, width, x, mask, w1, w2, w3, out, v3, h1, h2, s1, s2, h1s, h2s):
    forward_part(rows, width, x, mask, w1, w2, w3, out, v3, h1, h2, s1, s2, h1s, h2s)


def late_kernel(
    rows, width, x, cot, mask, w1, w2, w3, w1b, w2b, w3b, out, adj, tf, tm, tl,
    v3, s1, s2, h1s, h2s, c3, g2s, g1s,
):
    forward_part(rows, width, x, mask, w1, w2, w3, out, v3, None, None, s1, s2, h1s, h2s)
    hid, band = s1.shape[0], rows * width
    h1 = h1s.at[hid : 2 * hid, 6 * width : 6 * width + band]
    h2 = h2s.at[hid : 2 * hid, 4 * width : 4 * width + band]
    backward_part(rows, width, cot, mask, w1b, w2b, w3b, v3, h1, h2, s1, s2, adj, tf, tm, tl, c3, g2s, g1s)


def early_backward_kernel(
    rows, width, cot, mask, w1b, w2b, w3b, v3, h1, h2, s1, s2, adj, tf, tm, tl, c3, g2s, g1s
):
    backward_part(rows, width, cot, mask, w1b, w2b, w3b, v3, h1, h2, s1, s2, adj, tf, tm, tl, c3, g2s, g1s)


def greet(peers):
    barrier = pltpu.get_barrier_semaphore()
    total = jnp.int32(0)
    for present, peer in peers:
        @pl.when(present)
        def _(peer=peer):
            pl.semaphore_signal(barrier, inc=1, device_id=peer, device_id_type=MESH)

        total = total + present.astype(jnp.int32)
    pl.semaphore_wait(barrier, total)


def lay_out_weights(kf, km, kl, w1, w2, w3, w1b, w2b, w3b):
    taps, ch, hid = kf.shape
    spare = w3.shape[0] - ch

    def tall(kernel):
        block = [kernel[t].astype(F32) for t in range(taps)]
        if kernel.shape[1] == ch and spare:
            block = [jnp.concatenate([b, jnp.zeros((spare, hid), F32)], axis=0) for b in block]
        return block

    first, mid, last = tall(kf), tall(km), tall(kl)
    for block, across, along in ((first, w1, w1b), (mid, w2, w2b), (last, w3b, w3)):
        across[...] = jnp.transpose(jnp.concatenate(block, axis=0)).astype(BF)
        along[...] = jnp.concatenate(block, axis=1).astype(BF)


def halo_kernel(
    rows, width, lats, state, new, late, early, kf, km, kl, state_w, new_w, late_w, early_w,
    w1, w2, w3, w1b, w2b, w3b, low, high, send, recv,
):
    lat = lax.axis_index("lat")
    step = lax.axis_index("step")
    band, edge = rows * width, HALO * width
    ch = state.shape[0]
    has_low, has_high = lat > 0, lat < lats - 1
    greet([(has_low, {"lat": lat - 1}), (has_high, {"lat": lat + 1})])
    blocks = ((state, state_w), (new, new_w), (late, late_w), (early, early_w))

    def guarded(n, present):
        return (present & (step == 0)) if n == 1 else present

    ups, downs = [], []
    for n, (block, wide) in enumerate(blocks):
        ups.append(pltpu.make_async_remote_copy(
            src_ref=block.at[:, band - edge :], dst_ref=low.at[n], send_sem=send.at[2 * n], recv_sem=recv.at[2 * n],
            device_id={"lat": lat + 1}, device_id_type=MESH,
        ))
        downs.append(pltpu.make_async_remote_copy(
            src_ref=block.at[:, :edge], dst_ref=high.at[n], send_sem=send.at[2 * n + 1],
            recv_sem=recv.at[2 * n + 1], device_id={"lat": lat - 1}, device_id_type=MESH,
        ))
        pl.when(guarded(n, has_high))(ups[n].start)
        pl.when(guarded(n, has_low))(downs[n].start)
    for n, (block, wide) in enumerate(blocks):
        wide[:ch, edge : edge + band] = block[...]
        wide[:ch, :edge] = jnp.zeros((ch, edge), BF)
        wide[:ch, edge + band :] = jnp.zeros((ch, edge), BF)
        wide[ch:, :] = jnp.zeros((wide.shape[0] - ch, band + 2 * edge), BF)
    lay_out_weights(kf, km, kl, w1, w2, w3, w1b, w2b, w3b)
    for n, (block, wide) in enumerate(blocks):
        @pl.when(guarded(n, has_low))
        def _(n=n, wide=wide):
            ups[n].wait_recv()
            wide[:ch, :edge] = low[n]

        @pl.when(guarded(n, has_high))
        def _(n=n, wide=wide):
            downs[n].wait_recv()
            wide[:ch, edge + band :] = high[n]

        pl.when(guarded(n, has_high))(ups[n].wait_send)
        pl.when(guarded(n, has_low))(downs[n].wait_send)


def step_kernel(rows, width, steps, lats, distance, adds, block, base, out, got, send, recv):
    lat = lax.axis_index("lat")
    step = lax.axis_index("step")
    band, edge = rows * width, HALO * width

    def present(s, l):
        return (s >= 0) & (s < steps) & (l >= 0) & (l < lats)

    peers = []
    for s in (step - 1, step + 1):
        for l in (lat - 1, lat, lat + 1):
            peers.append((present(s, l), {"step": s, "lat": l}))
    greet(peers)
    moves = []
    for n, (shift, source, target) in enumerate((
        (1, pl.ds(band - edge, edge), pl.ds(0, edge)),
        (0, pl.ds(0, band), pl.ds(edge, band)),
        (-1, pl.ds(0, edge), pl.ds(edge + band, edge)),
    )):
        copy = pltpu.make_async_remote_copy(
            src_ref=block.at[:, source], dst_ref=got.at[:, target], send_sem=send.at[n], recv_sem=recv.at[n],
            device_id={"step": step + distance, "lat": lat + shift}, device_id_type=MESH,
        )
        pl.when(present(step + distance, lat + shift))(copy.start)
        moves.append((shift, target, copy))
    for shift, target, copy in moves:
        arrives = present(step - distance, lat - shift)

        @pl.when(arrives)
        def _(target=target, copy=copy):
            copy.wait_recv()
            if adds:
                out[:, target] = (base[:, target].astype(F32) + got[:, target].astype(F32)).astype(BF)
            else:
                out[:, target] = got[:, target]

        @pl.when(jnp.logical_not(arrives))
        def _(target=target):
            if adds:
                out[:, target] = base[:, target]
            else:
                first = (step == 0).astype(F32)
                out[:, target] = (base[:, target].astype(F32) * first).astype(BF)

        pl.when(present(step + distance, lat + shift))(copy.wait_send)


def reduce_kernel(
    pairs, lats, piece, scale, *refs
):
    terms, out = refs[:6], refs[6]
    src, got_a, part_b, got_b, part_c, got_c, full, send, recv = refs[7:]
    late_first, late_mid, late_last, early_first, early_mid, early_last = terms
    step = lax.axis_index("step")
    lat = lax.axis_index("lat")
    core = lax.rem(step, 2)
    pair = step // 2
    half, wedge = pairs * lats * piece, lats * piece
    segments = got_a.shape[0]

    partner = {"step": pair * 2 + (1 - core)}

    def pair_peer(k):
        return {"step": lax.rem(pair + k, pairs) * 2 + core}

    def lat_peer(k):
        return {"lat": lax.rem(lat + k, lats)}

    peers = [partner]
    peers += [pair_peer(k) for k in range(1, pairs)]
    peers += [lat_peer(k) for k in range(1, lats)]
    barrier = pltpu.get_barrier_semaphore()
    for peer in peers:
        pl.semaphore_signal(barrier, inc=1, device_id=peer, device_id_type=MESH)

    cp, hid = late_first.shape[1], late_mid.shape[1]
    lane = src.shape[1]
    rest = hid - lane
    tap_rows = 3 * cp + hid + hid // 2
    taps = late_first.shape[0]

    @pl.loop(0, taps)
    def _(t):
        start = pl.multiple_of(t * tap_rows, 16)
        first = late_first[t] + early_first[t]
        last = late_last[t] + early_last[t]
        mid = late_mid[t] + early_mid[t]
        src[pl.ds(start, cp), :] = first[:, :lane].astype(BF)
        src[pl.ds(start + cp, cp), :] = last[:, :lane].astype(BF)
        src[pl.ds(start + 2 * cp, cp), :] = jnp.concatenate([first[:, lane:], last[:, lane:]], axis=1).astype(BF)
        src[pl.ds(start + 3 * cp, hid), :] = mid[:, :lane].astype(BF)
        src[pl.ds(start + 3 * cp + hid, hid // 2), :] = jnp.concatenate(
            [mid[: hid // 2, lane:], mid[hid // 2 :, lane:]], axis=1
        ).astype(BF)

    used = taps * tap_rows
    if used < src.shape[0]:
        src[used:, :] = jnp.zeros((src.shape[0] - used, lane), BF)
    pl.semaphore_wait(barrier, len(peers))

    count = [0]

    def rows_at(start, size):
        return pl.ds(pl.multiple_of(start, 16), size)

    def copy(source, target, peer):
        slot = count[0]
        count[0] += 1
        made = pltpu.make_async_remote_copy(
            src_ref=source, dst_ref=target, send_sem=send.at[slot], recv_sem=recv.at[slot],
            device_id=peer, device_id_type=MESH,
        )
        made.start()
        return made

    def finish(copies):
        for made in copies:
            made.wait()

    def stage_b(q):
        base = q * 2 * half + core * half
        for b in range(pairs):
            mine = src[rows_at(base + b * wedge, wedge), :].astype(F32)
            theirs = got_a[q, b * wedge : (b + 1) * wedge, :].astype(F32)
            part_b[q, b * wedge : (b + 1) * wedge, :] = (mine + theirs).astype(BF)
        return [
            copy(part_b.at[q, rows_at(lax.rem(pair + k, pairs) * wedge, wedge)], got_b.at[q, k - 1], pair_peer(k))
            for k in range(1, pairs)
        ]

    def stage_c(q):
        base = q * 2 * half + core * half + pair * wedge
        for c in range(lats):
            total = src[rows_at(base + c * piece, piece), :].astype(F32)
            total = total + got_a[q, rows_at(pair * wedge + c * piece, piece), :].astype(F32)
            for k in range(pairs - 1):
                total = total + got_b[q, k, c * piece : (c + 1) * piece, :].astype(F32)
            part_c[q, c * piece : (c + 1) * piece, :] = total.astype(BF)
        return [
            copy(part_c.at[q, rows_at(lax.rem(lat + k, lats) * piece, piece)], got_c.at[q, k - 1], lat_peer(k))
            for k in range(1, lats)
        ]

    def spread_c(q):
        total = part_c[q, rows_at(lat * piece, piece), :].astype(F32)
        for k in range(lats - 1):
            total = total + got_c[q, k].astype(F32)
        mine = rows_at(q * 2 * half + core * half + pair * wedge + lat * piece, piece)
        full[mine, :] = (total * scale).astype(BF)
        return [copy(full.at[mine], full.at[mine], lat_peer(k)) for k in range(1, lats)]

    def spread_b(q):
        held = full.at[rows_at(q * 2 * half + core * half + pair * wedge, wedge)]
        return [copy(held, held, pair_peer(k)) for k in range(1, pairs)]

    def spread_a(q):
        held = full.at[rows_at(q * 2 * half + core * half, half)]
        return [copy(held, held, partner)]

    flying = [
        [copy(src.at[rows_at(q * 2 * half + (1 - core) * half, half)], got_a.at[q], partner)]
        for q in range(segments)
    ]
    for stage in (stage_b, stage_c, spread_c, spread_b, spread_a):
        for q in range(segments):
            finish(flying[q])
            flying[q] = stage(q)
    for q in range(segments):
        finish(flying[q])
    out[...] = full[...]


def unpack_kernel(packed, out_first, out_mid, out_last):
    ch, hid = out_first.shape[1:]
    lane = packed.shape[1]
    rest = hid - lane
    cp = (packed.shape[0] - hid - hid // 2) // 3
    tails = packed[2 * cp : 3 * cp, :].astype(F32)
    out_first[0, :, :lane] = packed[:cp, :].astype(F32)[:ch]
    out_first[0, :, lane:] = tails[:ch, :rest]
    out_last[0, :, :lane] = packed[cp : 2 * cp, :].astype(F32)[:ch]
    out_last[0, :, lane:] = tails[:ch, rest:]
    tails = packed[3 * cp + hid :, :].astype(F32)
    out_mid[0, :, :lane] = packed[3 * cp : 3 * cp + hid, :].astype(F32)
    out_mid[0, : hid // 2, lane:] = tails[:, :rest]
    out_mid[0, hid // 2 :, lane:] = tails[:, rest:]


def all_reduce(late_terms, early_terms, ch, scale):
    pairs = lax.axis_size("step") // 2
    lats = lax.axis_size("lat")
    pieces = 2 * pairs * lats
    taps, cp, hid = late_terms[0].shape
    lane = 128
    tap_rows = 3 * cp + hid + hid // 2
    segments = 2
    piece = -(-taps * tap_rows // (segments * pieces * 16)) * 16
    rows = segments * pieces * piece
    copies = segments * (2 + 2 * (pairs - 1) + 2 * (lats - 1))
    vmem = pl.BlockSpec(memory_space=pltpu.VMEM)
    packed = pl.pallas_call(
        functools.partial(reduce_kernel, pairs, lats, piece, scale),
        out_shape=jax.ShapeDtypeStruct((rows, lane), BF),
        in_specs=[vmem] * 6,
        out_specs=vmem,
        scratch_shapes=[
            pltpu.VMEM((rows, lane), BF),
            pltpu.VMEM((segments, pairs * lats * piece, lane), BF),
            pltpu.VMEM((segments, pairs * lats * piece, lane), BF),
            pltpu.VMEM((segments, max(pairs - 1, 1), lats * piece, lane), BF),
            pltpu.VMEM((segments, lats * piece, lane), BF),
            pltpu.VMEM((segments, max(lats - 1, 1), piece, lane), BF),
            pltpu.VMEM((rows, lane), BF),
            pltpu.SemaphoreType.DMA((copies,)),
            pltpu.SemaphoreType.DMA((copies,)),
        ],
        compiler_params=pltpu.CompilerParams(collective_id=0, has_side_effects=True),
        name="kernel_term_sum",
    )(*late_terms, *early_terms)
    return pl.pallas_call(
        unpack_kernel,
        grid=(taps,),
        out_shape=[
            jax.ShapeDtypeStruct((taps, ch, hid), F32),
            jax.ShapeDtypeStruct((taps, hid, hid), F32),
            jax.ShapeDtypeStruct((taps, ch, hid), F32),
        ],
        in_specs=[pl.BlockSpec((tap_rows, lane), lambda t: (t, 0))],
        out_specs=[
            pl.BlockSpec((1, ch, hid), lambda t: (t, 0, 0)),
            pl.BlockSpec((1, hid, hid), lambda t: (t, 0, 0)),
            pl.BlockSpec((1, ch, hid), lambda t: (t, 0, 0)),
        ],
        name="unpack_terms",
    )(packed)


def body(state_in, new_state, cot_early, cot_late, kernel_first, kernel_mid, kernel_last):
    steps, lats = lax.axis_size("step"), lax.axis_size("lat")
    ch, rows, width = new_state.shape
    hid = kernel_mid.shape[1]
    cp = -(-ch // 16) * 16
    band, edge = rows * width, HALO * width
    lat = lax.axis_index("lat")

    ext_row = lat * rows + jnp.arange(rows + 2 * HALO, dtype=jnp.int32) - HALO
    inside = (ext_row >= 0) & (ext_row < rows * lats)
    mask = jnp.repeat(inside.astype(F32), width)[None]

    vmem_spec = pl.BlockSpec(memory_space=pltpu.VMEM)
    wide_shape = jax.ShapeDtypeStruct((cp, band + 2 * edge), BF)
    weight_shapes = [
        jax.ShapeDtypeStruct(dims, BF)
        for dims in ((hid, 9 * cp), (hid, 9 * hid), (cp, 9 * hid), (cp, 9 * hid), (hid, 9 * hid), (hid, 9 * cp))
    ]
    state_w, new_w, late_cot_w, early_cot_w, w1, w2, w3, w1b, w2b, w3b = pl.pallas_call(
        functools.partial(halo_kernel, rows, width, lats),
        out_shape=[wide_shape] * 4 + weight_shapes,
        in_specs=[vmem_spec] * 7,
        out_specs=[vmem_spec] * 10,
        scratch_shapes=[
            pltpu.VMEM((4, ch, edge), BF), pltpu.VMEM((4, ch, edge), BF),
            pltpu.SemaphoreType.DMA((8,)), pltpu.SemaphoreType.DMA((8,)),
        ],
        compiler_params=pltpu.CompilerParams(collective_id=1, has_side_effects=True),
        name="halos",
    )(
        *(block.reshape(ch, band) for block in (state_in[0], new_state, cot_late[0], cot_early[0])),
        kernel_first, kernel_mid, kernel_last,
    )

    def to_step(block, base, distance, adds):
        return pl.pallas_call(
            functools.partial(step_kernel, rows, width, steps, lats, distance, adds),
            out_shape=wide_shape,
            in_specs=[vmem_spec] * 2,
            out_specs=vmem_spec,
            scratch_shapes=[
                pltpu.VMEM(wide_shape.shape, BF),
                pltpu.SemaphoreType.DMA((3,)), pltpu.SemaphoreType.DMA((3,)),
            ],
            compiler_params=pltpu.CompilerParams(collective_id=3 if adds else 2, has_side_effects=True),
            name="step_cotangent" if adds else "step_state",
        )(block, base)

    vmem = pl.BlockSpec(memory_space=pltpu.VMEM)
    shape = jax.ShapeDtypeStruct
    lanes_v, lanes_1, lanes_2 = (rows + 14) * width, (rows + 12) * width, (rows + 8) * width
    saved_shapes = [
        ((3 * cp, lanes_v), BF), ((hid, band), BF), ((hid, band), BF),
        ((hid, lanes_1), BF), ((hid, lanes_2), BF),
    ]
    fwd_scratch = [((3 * hid, lanes_1), BF), ((3 * hid, lanes_2), BF)]
    bwd_scratch = [
        ((3 * cp, lanes_v), BF), ((3 * hid, (rows + 6) * width), BF), ((3 * hid, (rows + 2) * width), BF)
    ]
    bwd_outs = [
        ((cp, band), BF), ((3, 3 * cp, hid), F32), ((3, 3, hid, hid), F32), ((3, 3 * cp, hid), F32)
    ]

    def call(kernel, name, ins, outs, scratch):
        return pl.pallas_call(
            functools.partial(kernel, rows, width),
            out_shape=[shape(*o) for o in outs],
            in_specs=[vmem] * len(ins),
            out_specs=[vmem] * len(outs),
            scratch_shapes=[pltpu.VMEM(*s) for s in scratch],
            compiler_params=pltpu.CompilerParams(vmem_limit_bytes=56 * 1024 * 1024),
            name=name,
        )(*ins)

    early_out, *saved = call(
        early_forward_kernel, "early_forward", (state_w, mask, w1, w2, w3),
        [((cp, band), BF)] + saved_shapes, fwd_scratch,
    )
    late_in = to_step(early_out, new_w, 1, False)
    late_out, late_adj, *late_terms = call(
        late_kernel, "late_both", (late_in, late_cot_w, mask, w1, w2, w3, w1b, w2b, w3b),
        [((cp, band), BF)] + bwd_outs, saved_shapes[:1] + saved_shapes[3:] + fwd_scratch + bwd_scratch,
    )
    early_cot = to_step(late_adj, early_cot_w, -1, True)
    state_adj, *early_terms = call(
        early_backward_kernel, "early_backward", (early_cot, mask, w1b, w2b, w3b, *saved),
        bwd_outs, bwd_scratch,
    )

    def by_tap(terms):
        first, mid, last = terms
        return first.reshape(9, cp, hid), mid.reshape(9, hid, hid), last.reshape(9, cp, hid)

    scale = 1.0 / math.sqrt(2.0 * steps * rows * lats * width)
    first, mid, last = all_reduce(by_tap(late_terms), by_tap(early_terms), ch, scale)
    return (
        late_out[:ch].reshape(1, ch, rows, width),
        state_adj[:ch].reshape(1, ch, rows, width),
        first,
        mid,
        last,
    )


def solution(mesh):
    banded = P("step", None, "lat", None)
    return jax.shard_map(
        body,
        mesh=mesh,
        in_specs=(banded, P(None, "lat", None), banded, banded, P(), P(), P()),
        out_specs=(banded, banded, P(), P(), P()),
        check_vma=False,
    )
```
